512 devices in a mesh: ctx: 128 (over z, y, core), head: 4 (over x).
Axes of the slice: x: 4, y: 4, z: 16, core: 2. Of those that a mesh axis runs over, the one named last changes fastest.
Arguments:
- layer_input: bfloat16 [32768, 2048], P('ctx', 'head'), may hold values from -24 to 24
- queries: bfloat16 [32768, 1024], P('ctx', 'head'), may hold values from -6 to 6
- keys: bfloat16 [32768, 512], P('ctx', 'head'), may hold values from -6 to 6
- values: bfloat16 [32768, 512], P('ctx', 'head'), may hold values from -6 to 6
- result_cotangent: bfloat16 [32768, 1024], P('ctx', 'head'), may hold values from -0.3125 to 0.3125
- log_decay: float32 [4, 32768], P('head', 'ctx'), may hold values from -2 to 0
Outputs:
- weight_k_grad: bfloat16 [2048, 512], P('ctx', 'head')
- weight_v_grad: bfloat16 [2048, 512], P('ctx', 'head')
The draws below stay inside these ranges and needn't reach their ends.
All inputs are finite; a program needn't handle non-finite values.
Results may differ from the reference program's by a relative error of at most 0.0057.
Values may be sent and summed in bfloat16 or wider, within the bound.
No kernel may reach another device: no remote copies, remote signals or barrier semaphores. Data moves between devices by JAX's collectives and lax.ppermute only.
A program may use at most 64 MiB of HBM per device.

```python
import math
import jax
import jax.numpy as jnp
from jax import lax

D = 2048
HQ = 8
HK = 4
E = 128
WINDOW = 256
TOK_DEV = 256
TOKENS = 32768


def pair_draw(key):
    base = jax.random.fold_in(key, 7)
    key_q, key_k = jax.random.split(base, 2)
    query_draw = jax.random.truncated_normal(key_q, -6.0, 6.0, (TOKENS, HQ * E), jnp.float32)
    key_draw = jax.random.truncated_normal(key_k, -6.0, 6.0, (TOKENS, HK * E), jnp.float32)
    return (query_draw, key_draw)


def draw_queries(key, part):
    return pair_draw(key)[0].astype(jnp.bfloat16)


def draw_keys(key, part):
    return pair_draw(key)[1].astype(jnp.bfloat16)


def draw_log_decay(key, part):
    base = jax.random.fold_in(key, 11)
    key_order, key_slow, key_fast, key_device, key_rough, key_spot, dropout_key_seed = jax.random.split(base, 7)
    order = jax.random.permutation(key_order, HK)
    fast_count = HK // 2
    fast_heads = (order < fast_count)[:, None]
    slow_rate = jax.random.uniform(key_slow, (HK, 1), jnp.float32, 0.2, 0.4) / TOKENS
    fast_rate = jax.random.uniform(key_fast, (HK, 1), jnp.float32, 0.02, 0.04)
    arrival_frequency = jnp.where(fast_heads, fast_rate, slow_rate)
    block_count = TOKENS // TOK_DEV
    shard_among_cards = jnp.exp(jax.random.uniform(key_device, (HK, block_count), jnp.float32, 0.0, math.log(2.5)))
    shard_among_cards = jnp.repeat(shard_among_cards, TOK_DEV, axis=1)
    boundary_perturbation = jax.random.uniform(key_rough, (HK, TOKENS), jnp.float32, 0.5, 1.5)
    spots = jax.random.randint(key_spot, (HK, 2), 0, TOKENS)
    discarded_arrivals = jnp.log(1.0 - jax.random.uniform(dropout_key_seed, (HK, 2), jnp.float32, 0.2, 0.4))
    paired_arrivals = jnp.arange(TOKENS)[None, None, :] == spots[:, :, None]
    clustered_arrivals = jnp.sum(jnp.where(paired_arrivals, discarded_arrivals[:, :, None], 0.0), axis=1)
    return (-arrival_frequency * shard_among_cards * boundary_perturbation + clustered_arrivals).astype(jnp.float32)


def raised(drawn, key, source, target, parts, factor):
    owner, partner = [(jnp.arange(drawn.shape[axis_at]) // (drawn.shape[axis_at] // parts)).reshape([-1 if axis == axis_at else 1 for axis in range(drawn.ndim)]) for axis_at in (source, target)]
    chosen = jax.random.permutation(key, parts)[partner]
    strong = (owner == chosen) | (owner == (partner + parts // 2) % parts)
    return jnp.where(strong, factor * drawn, drawn)


def block_levels(stream_key, extent, cuts, low, largest):
    level = 1.0
    for axis_at, shards_of in cuts:
        draws = jax.random.uniform(jax.random.fold_in(jax.random.fold_in(stream_key, 6), axis_at), (shards_of,), jnp.float32, low / len(cuts), largest / len(cuts))
        level = level * jnp.repeat(jnp.exp(draws), extent[axis_at] // shards_of).reshape((-1,) + (1,) * (len(extent) - 1 - axis_at))
    return level


def gaussian(rng, dims, deviation, reach, pieces=(), kind=jnp.bfloat16):
    result = jax.random.normal(rng, dims, jnp.float32) * deviation
    if len(pieces) > 0:
        result = block_levels(rng, dims, pieces, -0.22, 0.18) * result
    return jnp.clip(result, min=-reach, max=reach).astype(kind)


def bell_draw_with(rng, dims, width, bound, cuts, heavy, kind=jnp.bfloat16):
    array = width * jax.random.normal(rng, dims, jnp.float32)
    if cuts:
        array = array * block_levels(rng, dims, cuts, -0.22, 0.18)
    return jnp.clip(raised(array, jax.random.fold_in(rng, 3), *heavy), -bound, bound).astype(kind)


def setup_inputs(seed: int = 0) -> dict:
    splits = jax.random.split(jax.random.key(seed), 7)
    return {
        "layer_input": bell_draw_with(splits[0], (TOKENS, D), 1.0, 24.0, ((0, 128), (1, 4)), (0, 1, 128, 5.5)),
        "queries": draw_queries(jax.random.fold_in(splits[6], 71), 0),
        "keys": draw_keys(jax.random.fold_in(splits[6], 71), 0),
        "values": gaussian(splits[3], (TOKENS, HK * E), 1.0, 6.0, ((0, 128), (1, 4))),
        "result_cotangent": gaussian(splits[4], (TOKENS, HQ * E), 0.02, 0.3125, ((0, 128), (1, 4))),
        "log_decay": draw_log_decay(jax.random.fold_in(splits[6], 71), 0),
    }


neg_fill = -1e+30

def rounded(value):
    return lax.optimization_barrier(value.astype(jnp.bfloat16)).astype(jnp.float32)

def band_terms(q_rows, h_rows, k_rows, v_rows, query_pos, key_pos):
    factor = 1.0 / math.sqrt(E)
    scores = jnp.einsum('tgrd,jgd->grtj', q_rows, k_rows) * factor
    offset = query_pos[:, None] - key_pos[None, :]
    inside = (offset >= 0) & (offset < WINDOW) & (key_pos[None, :] >= 0)
    scores = jnp.where(inside, scores, neg_fill)
    row_max = lax.optimization_barrier(jnp.max(scores, axis=3, keepdims=True))
    expo = jnp.exp(scores - row_max)
    attend = expo / lax.optimization_barrier(jnp.sum(expo, axis=3, keepdims=True))
    attend_low = rounded(attend)
    dprob = jnp.einsum('tgrd,jgd->grtj', h_rows, v_rows)
    row_delta = lax.optimization_barrier(jnp.sum(attend * dprob, axis=3, keepdims=True))
    dscore = rounded(attend * (dprob - row_delta))
    key_part = jnp.einsum('grtj,tgrd->jgd', dscore, q_rows) * factor
    value_part = jnp.einsum('grtj,tgrd->jgd', attend_low, h_rows)
    return (key_part, value_part)

def reference(layer_input, queries, keys, values, result_cotangent, log_decay):
    group_size = HQ // HK
    block_count = TOKENS // TOK_DEV
    lin_scale = 1.0 / (32 * E)
    q_all = queries.astype(jnp.float32).reshape(TOKENS, HK, group_size, E)
    h_all = (result_cotangent * 0.5).astype(jnp.float32).reshape(TOKENS, HK, group_size, E)
    k_all = keys.astype(jnp.float32).reshape(TOKENS, HK, E)
    v_all = values.astype(jnp.float32).reshape(TOKENS, HK, E)
    log_sums = jnp.cumsum(log_decay.astype(jnp.float32).reshape(HK, block_count, TOK_DEV), axis=2)

    def summary(block_index):
        row_start = (block_index * TOK_DEV).astype(jnp.int32)
        q_block = lax.dynamic_slice_in_dim(q_all, row_start, TOK_DEV, 0)
        h_block = lax.dynamic_slice_in_dim(h_all, row_start, TOK_DEV, 0)
        sums_block = log_sums[:, block_index]
        weighted = rounded(jnp.exp(sums_block).T[:, :, None, None] * h_block)
        grad_block = jnp.einsum('tgrd,tgre->gde', q_block, weighted) * lin_scale
        return (grad_block, jnp.exp(sums_block[:, -1]))
    block_grads, block_decays = lax.map(summary, jnp.arange(block_count, dtype=jnp.int32))

    def backward_step(incoming, inputs):
        grad_block, decay_block = inputs
        return (grad_block + decay_block[:, None, None] * incoming, incoming)
    _, carries = lax.scan(backward_step, jnp.zeros((HK, E, E), jnp.float32), (block_grads, block_decays), reverse=True)
    q_pad = jnp.pad(q_all, ((WINDOW, WINDOW), (0, 0), (0, 0), (0, 0)))
    h_pad = jnp.pad(h_all, ((WINDOW, WINDOW), (0, 0), (0, 0), (0, 0)))
    k_pad = jnp.pad(k_all, ((WINDOW, WINDOW), (0, 0), (0, 0)))
    v_pad = jnp.pad(v_all, ((WINDOW, WINDOW), (0, 0), (0, 0)))

    def block_work(inputs):
        block_index, incoming = inputs
        row_start = (block_index * TOK_DEV).astype(jnp.int32)
        own_q = lax.dynamic_slice_in_dim(q_pad, row_start + WINDOW, TOK_DEV, 0)
        own_h = lax.dynamic_slice_in_dim(h_pad, row_start + WINDOW, TOK_DEV, 0)
        own_k = lax.dynamic_slice_in_dim(k_pad, row_start, TOK_DEV + WINDOW, 0)
        own_v = lax.dynamic_slice_in_dim(v_pad, row_start, TOK_DEV + WINDOW, 0)
        query_pos = row_start + jnp.arange(TOK_DEV, dtype=jnp.int32)
        key_pos = row_start - WINDOW + jnp.arange(TOK_DEV + WINDOW, dtype=jnp.int32)
        win_k, win_v = band_terms(own_q, own_h, own_k, own_v, query_pos, key_pos)
        next_q = lax.dynamic_slice_in_dim(q_pad, row_start + TOK_DEV + WINDOW, WINDOW, 0)
        next_h = lax.dynamic_slice_in_dim(h_pad, row_start + TOK_DEV + WINDOW, WINDOW, 0)
        next_k = lax.dynamic_slice_in_dim(k_pad, row_start + TOK_DEV, 2 * WINDOW, 0)
        next_v = lax.dynamic_slice_in_dim(v_pad, row_start + TOK_DEV, 2 * WINDOW, 0)
        next_qpos = row_start + TOK_DEV + jnp.arange(WINDOW, dtype=jnp.int32)
        next_kpos = row_start + TOK_DEV - WINDOW + jnp.arange(2 * WINDOW, dtype=jnp.int32)
        edge_k, edge_v = band_terms(next_q, next_h, next_k, next_v, next_qpos, next_kpos)
        zero_rows = jnp.zeros((TOK_DEV - WINDOW, HK, E), jnp.float32)
        win_k = win_k[WINDOW:] + jnp.concatenate([zero_rows, edge_k[:WINDOW]], axis=0)
        win_v = win_v[WINDOW:] + jnp.concatenate([zero_rows, edge_v[:WINDOW]], axis=0)
        k_block = own_k[WINDOW:]
        v_block = own_v[WINDOW:]
        sums_block = log_sums[:, block_index]
        row_after = lax.broadcasted_iota(jnp.int32, (TOK_DEV, TOK_DEV), 0)
        row_before = lax.broadcasted_iota(jnp.int32, (TOK_DEV, TOK_DEV), 1)
        mixing = jnp.exp(jnp.where(row_after >= row_before, sums_block[:, :, None] - sums_block[:, None, :], neg_fill))
        key_mix = rounded(mixing[:, None] * jnp.einsum('tgrd,jgd->grtj', own_h, v_block))
        value_mix = rounded(mixing[:, None] * jnp.einsum('tgrd,jgd->grtj', own_q, k_block))
        lin_k = jnp.einsum('grtj,tgrd->jgd', key_mix, own_q) * lin_scale
        lin_v = jnp.einsum('grtj,tgrd->jgd', value_mix, own_h) * lin_scale
        tail_decay = jnp.exp(sums_block[:, -1:] - sums_block).T[:, :, None]
        lin_k = lin_k + tail_decay * jnp.einsum('tgj,gij->tgi', v_block, incoming, precision=lax.Precision.HIGHEST)
        lin_v = lin_v + tail_decay * jnp.einsum('tgi,gij->tgj', k_block, incoming, precision=lax.Precision.HIGHEST)
        key_grad = (lin_k + win_k).astype(jnp.bfloat16).reshape(TOK_DEV, HK * E)
        value_grad = (lin_v + win_v).astype(jnp.bfloat16).reshape(TOK_DEV, HK * E)
        return (key_grad, value_grad)
    key_blocks, content_tiles = lax.map(block_work, (jnp.arange(block_count, dtype=jnp.int32), carries))
    key_grad = key_blocks.reshape(TOKENS, HK * E)
    value_grad = content_tiles.reshape(TOKENS, HK * E)
    weight_k_grad = jnp.dot(layer_input.T, key_grad, preferred_element_type=jnp.float32).astype(jnp.bfloat16)
    weight_v_grad = jnp.dot(layer_input.T, value_grad, preferred_element_type=jnp.float32).astype(jnp.bfloat16)
    return (weight_k_grad, weight_v_grad)
```

```python
import jax
import jax.numpy as jnp
from jax import lax
from jax.sharding import Mesh, PartitionSpec as P

E = 128
WINDOW = 256
NZ, NY, NC = 16, 4, 2
NP = NY * NC

neg_fill = -1e30

PLANE = ("y", "core")
CTX = ("z", "y", "core")


def shifted(value, steps):
    count = NZ * NP
    leading, last = (max(0, -steps), min(count, count - steps))
    return lax.ppermute(value, CTX, [(source, source + steps) for source in range(leading, last)])


def band_grads(q_block, h_block, key_rows, value_rows, query_pos, key_pos):
    head_dim = key_rows.shape[1]
    group_size = q_block.shape[1] // head_dim
    row_count = q_block.shape[0]
    q_heads = q_block.reshape(row_count, group_size, head_dim)
    h_heads = h_block.reshape(row_count, group_size, head_dim)
    factor = head_dim ** (-0.5)
    scores = (
        jnp.einsum("trd,jd->rtj", q_heads, key_rows, preferred_element_type=jnp.float32) * factor
    )
    offset = query_pos[:, None] - key_pos[None, :]
    inside = (offset >= 0) & (offset < WINDOW) & (key_pos[None, :] >= 0)
    scores = jnp.where(inside[None], scores, neg_fill)
    row_max = jnp.max(scores, axis=2, keepdims=True)
    expo = jnp.exp(scores - row_max)
    attend = expo / jnp.sum(expo, axis=2, keepdims=True)
    attend_low = attend.astype(jnp.bfloat16)
    dprob = jnp.einsum("trd,jd->rtj", h_heads, value_rows, preferred_element_type=jnp.float32)
    row_delta = jnp.sum(attend * dprob, axis=2, keepdims=True)
    dscore = (attend * (dprob - row_delta)).astype(jnp.bfloat16)
    key_part = (
        jnp.einsum("rtj,trd->jd", dscore, q_heads, preferred_element_type=jnp.float32) * factor
    )
    value_part = jnp.einsum("rtj,trd->jd", attend_low, h_heads, preferred_element_type=jnp.float32)
    return (key_part, value_part)


def linear_terms(q_block, h_block, key_rows, value_rows, log_rates, lin_scale):
    head_dim = key_rows.shape[1]
    group_size = q_block.shape[1] // head_dim
    length = q_block.shape[0]
    q_heads = q_block.reshape(length, group_size, head_dim)
    h_heads = h_block.reshape(length, group_size, head_dim)
    log_sums = jnp.cumsum(log_rates)
    row_after = lax.broadcasted_iota(jnp.int32, (length, length), 0)
    row_before = lax.broadcasted_iota(jnp.int32, (length, length), 1)
    mixing = jnp.exp(
        jnp.where(row_after >= row_before, log_sums[:, None] - log_sums[None, :], neg_fill)
    )
    key_mix = (
        mixing[None]
        * jnp.einsum("trd,jd->rtj", h_heads, value_rows, preferred_element_type=jnp.float32)
    ).astype(jnp.bfloat16)
    value_mix = (
        mixing[None]
        * jnp.einsum("trd,jd->rtj", q_heads, key_rows, preferred_element_type=jnp.float32)
    ).astype(jnp.bfloat16)
    key_part = (
        jnp.einsum("rtj,trd->jd", key_mix, q_heads, preferred_element_type=jnp.float32) * lin_scale
    )
    value_part = (
        jnp.einsum("rtj,trd->jd", value_mix, h_heads, preferred_element_type=jnp.float32)
        * lin_scale
    )
    weighted = (jnp.exp(log_sums)[:, None, None] * h_heads).astype(jnp.bfloat16)
    block_grad = (
        jnp.einsum("trd,tre->de", q_heads, weighted, preferred_element_type=jnp.float32) * lin_scale
    )
    return (key_part, value_part, block_grad, log_sums)


def between(logs, first):
    count = logs.shape[0]
    i = lax.broadcasted_iota(jnp.int32, (count, count), 0)
    l = lax.broadcasted_iota(jnp.int32, (count, count), 1)
    total = jnp.sum(jnp.where((l > first) & (l < i), logs[None, :], 0.0), axis=1)
    return jnp.where(jnp.arange(count) > first, jnp.exp(total), 0.0)


def state_entering(block_grad, log_total):
    rows = E // NP
    tail = jnp.broadcast_to(log_total, (NP, 8, E))
    sent = jnp.concatenate([block_grad.reshape(NP, rows, E), tail], axis=1)
    got = lax.all_to_all(sent, PLANE, 0, 0, tiled=True)
    grads, logs = got[:, :rows], got[:, rows, 0]
    inner = jnp.stack([between(logs, k) for k in range(-1, NP)])
    own = jnp.einsum("kl,lrd->krd", inner, grads, precision=lax.Precision.HIGHEST)
    plane_log = jnp.sum(logs)
    out = jnp.concatenate([own[0], jnp.broadcast_to(plane_log, (8, E))], axis=0)
    planes = lax.all_to_all(
        jnp.broadcast_to(out[None], (NZ, rows + 8, E)), "z", 0, 0, tiled=True
    )
    weights = between(planes[:, rows, 0], lax.axis_index("z"))
    later = jnp.sum(weights[:, None, None] * planes[:, :rows], axis=0)
    k = lax.broadcasted_iota(jnp.int32, (NP, NP), 0)
    l = lax.broadcasted_iota(jnp.int32, (NP, NP), 1)
    after = jnp.exp(jnp.sum(jnp.where(l > k, logs[None, :], 0.0), axis=1))
    entering = own[1:] + after[:, None, None] * later[None]
    back = lax.all_to_all(entering, PLANE, 0, 0, tiled=True)
    return back.reshape(E, E)


def on_device(layer_input, queries, keys, values, result_cotangent, log_decay):
    length = queries.shape[0]
    head_dim = E
    lin_scale = 1.0 / (32 * head_dim)
    halves = result_cotangent * 0.5
    row_start = lax.axis_index(CTX) * length
    query_pos = row_start + jnp.arange(length, dtype=jnp.int32)
    key_pos = row_start - WINDOW + jnp.arange(length + WINDOW, dtype=jnp.int32)
    inputs = lax.all_gather(layer_input, "head", axis=1, tiled=True)
    prior = shifted(jnp.concatenate([keys, values], axis=1), 1)
    lin_k, lin_v, block_grad, log_sums = linear_terms(
        queries, halves, keys, values, log_decay[0], lin_scale
    )
    state_in = state_entering(block_grad, log_sums[-1])
    full_k = jnp.concatenate([prior[:, :head_dim], keys], axis=0)
    full_v = jnp.concatenate([prior[:, head_dim:], values], axis=0)
    win_k, win_v = band_grads(queries, halves, full_k, full_v, query_pos, key_pos)
    back = shifted(
        jnp.concatenate([win_k[:WINDOW], win_v[:WINDOW]], axis=1).astype(jnp.bfloat16), -1
    ).astype(jnp.float32)
    tail_decay = jnp.exp(log_sums[-1] - log_sums)[:, None]
    state_low = state_in.astype(jnp.bfloat16)
    lin_k = lin_k + tail_decay * lax.dot_general(
        values, state_low, (((1,), (1,)), ((), ())), preferred_element_type=jnp.float32
    )
    lin_v = lin_v + tail_decay * jnp.dot(keys, state_low, preferred_element_type=jnp.float32)
    key_grad = (lin_k + win_k[WINDOW:] + back[:, :head_dim]).astype(jnp.bfloat16)
    value_grad = (lin_v + win_v[WINDOW:] + back[:, head_dim:]).astype(jnp.bfloat16)
    both_grads = jnp.concatenate([key_grad, value_grad], axis=1)
    partial_value = lax.dot_general(
        inputs,
        both_grads,
        (((0,), (0,)), ((), ())),
        preferred_element_type=jnp.float32,
    ).astype(jnp.bfloat16)
    width = 2 * head_dim
    rows = partial_value.shape[0] // (NZ * NP)
    parts = partial_value.reshape(NZ, NP, rows, width).transpose(1, 0, 2, 3)
    parts = lax.all_to_all(parts, PLANE, 0, 0, tiled=True)
    parts = jnp.sum(parts.astype(jnp.float32), axis=0).astype(jnp.bfloat16)
    parts = lax.all_to_all(parts, "z", 0, 0, tiled=True)
    owned = jnp.sum(parts.astype(jnp.float32), axis=0)
    return (owned[:, :head_dim].astype(jnp.bfloat16), owned[:, head_dim:].astype(jnp.bfloat16))


def solution(mesh):
    fine = Mesh(mesh.devices.reshape(NZ, NY, NC, mesh.devices.shape[1]), CTX + ("head",))
    rows = P(CTX, "head")
    in_specs = (rows, rows, rows, rows, rows, P("head", CTX))
    return jax.shard_map(
        on_device, mesh=fine, in_specs=in_specs, out_specs=(rows, rows), check_vma=False
    )
```

```python
import jax
import jax.numpy as jnp
from jax import lax
from jax.experimental import pallas as pl
from jax.experimental.pallas import tpu as pltpu
from jax.sharding import Mesh, PartitionSpec as P

E = 128
LEN = 256
NZ, NY, NC = 16, 4, 2
NP = NY * NC
NH = 4
XD = 512
ROWS = E // NP
LIN = 1.0 / (32 * E)
FACTOR = E ** (-0.5)
F32, BF16 = jnp.float32, jnp.bfloat16

neg_fill = -1e30

PLANE = ("y", "core")
CTX = ("z", "y", "core")

NN = (((1,), (0,)), ((), ()))
NT = (((1,), (1,)), ((), ()))
TN = (((0,), (0,)), ((), ()))


def mm(a, b, dims):
    return lax.dot_general(a, b, dims, preferred_element_type=F32)


def vmem(count):
    return [pl.BlockSpec(memory_space=pltpu.VMEM)] * count


SMEM = pl.BlockSpec(memory_space=pltpu.SMEM)


def cost(flops, nbytes):
    return pl.CostEstimate(flops=flops, bytes_accessed=nbytes, transcendentals=0)


def params(mib):
    return pltpu.CompilerParams(vmem_limit_bytes=mib << 20)


def log_sums(ld):
    t = lax.broadcasted_iota(jnp.int32, (LEN, LEN), 0)
    u = lax.broadcasted_iota(jnp.int32, (LEN, LEN), 1)
    column = jnp.sum(jnp.where(u <= t, ld, 0.0), axis=1, keepdims=True)
    row = jnp.sum(jnp.where(u == t, column, 0.0), axis=0, keepdims=True)
    return column, row


def summary_kernel(q_ref, c_ref, ld_ref, out_ref):
    column, _ = log_sums(ld_ref[...])
    grow = jnp.exp(column)
    total = jnp.zeros((E, E), F32)
    for r in range(2):
        cols = slice(r * E, (r + 1) * E)
        half = c_ref[:, cols].astype(F32) * 0.5
        total += mm(q_ref[:, cols], (grow * half).astype(BF16), TN)
    last = jnp.broadcast_to(column[LEN - 1 :, :], (8, E))
    for m in range(NP):
        out_ref[m, :ROWS, :] = total[m * ROWS : (m + 1) * ROWS] * LIN
        out_ref[m, ROWS:, :] = last


def summary(q, c, ld):
    return pl.pallas_call(
        summary_kernel,
        out_shape=jax.ShapeDtypeStruct((NP, ROWS + 8, E), F32),
        in_specs=vmem(3),
        out_specs=vmem(1)[0],
        cost_estimate=cost(2 * LEN * E * E * 2, 400000),
        compiler_params=params(8),
        name="summary",
    )(q, c, ld)


def local_kernel(idx_ref, q_ref, c_ref, k_ref, v_ref, prior_ref, ld_ref, own_ref, back_ref):
    column, row = log_sums(ld_ref[...])
    j = lax.broadcasted_iota(jnp.int32, (LEN, LEN), 0)
    t = lax.broadcasted_iota(jnp.int32, (LEN, LEN), 1)
    inside = j <= t
    mixing = jnp.exp(jnp.where(inside, row - column, neg_fill))
    outside = jnp.where(idx_ref[0] > 0, 0.0, neg_fill)
    k, v = k_ref[...], v_ref[...]
    prior_k, prior_v = prior_ref[:, :E], prior_ref[:, E:]
    own_k, own_v = jnp.zeros((LEN, E), F32), jnp.zeros((LEN, E), F32)
    win_k, win_v = jnp.zeros((LEN, E), F32), jnp.zeros((LEN, E), F32)
    old_k, old_v = jnp.zeros((LEN, E), F32), jnp.zeros((LEN, E), F32)
    zero = jnp.zeros((LEN, LEN), BF16)
    for r in range(2):
        cols = slice(r * E, (r + 1) * E)
        q = q_ref[:, cols]
        half = (c_ref[:, cols].astype(F32) * 0.5).astype(BF16)
        raw = mm(k, q, NT)
        prod = mm(v, half, NT)
        scores = jnp.where(inside, raw * FACTOR, mm(prior_k, q, NT) * FACTOR + outside)
        dprob = jnp.where(inside, prod, mm(prior_v, half, NT))
        expo = jnp.exp(scores - jnp.max(scores, axis=0, keepdims=True))
        attend = expo / jnp.sum(expo, axis=0, keepdims=True)
        delta = jnp.sum(attend * dprob, axis=0, keepdims=True)
        dscore = (attend * (dprob - delta)).astype(BF16)
        low = attend.astype(BF16)
        own_k += mm((mixing * prod).astype(BF16), q, NN)
        own_v += mm((mixing * raw).astype(BF16), half, NN)
        win_k += mm(jnp.where(inside, dscore, zero), q, NN)
        win_v += mm(jnp.where(inside, low, zero), half, NN)
        old_k += mm(jnp.where(inside, zero, dscore), q, NN)
        old_v += mm(jnp.where(inside, zero, low), half, NN)
    own_ref[:, :E] = own_k * LIN + win_k * FACTOR
    own_ref[:, E:] = own_v * LIN + win_v
    back_ref[:, :E] = old_k * FACTOR
    back_ref[:, E:] = old_v


def local(idx, q, c, k, v, prior, ld):
    shape = jax.ShapeDtypeStruct((LEN, 2 * E), F32)
    return pl.pallas_call(
        local_kernel,
        out_shape=(shape, shape),
        in_specs=[SMEM] + vmem(6),
        out_specs=tuple(vmem(2)),
        cost_estimate=cost(2 * 20 * LEN * LEN * E, 1200000),
        compiler_params=params(16),
        name="local",
    )(idx, q, c, k, v, prior, ld)


def plane_kernel(got_ref, out_ref):
    log = jnp.zeros((8, E), F32)
    low, high = jnp.zeros((8, E), F32), jnp.zeros((8, E), F32)
    for k in range(NP):
        weight = jnp.exp(log)
        low += weight * got_ref[k, 0:8, :]
        high += weight * got_ref[k, 8:16, :]
        log += got_ref[k, ROWS:, :]
    for z in range(NZ):
        out_ref[z, 0:8, :] = low
        out_ref[z, 8:16, :] = high
        out_ref[z, ROWS:, :] = log


def plane_total(got):
    return pl.pallas_call(
        plane_kernel,
        out_shape=jax.ShapeDtypeStruct((NZ, ROWS + 8, E), F32),
        in_specs=vmem(1),
        out_specs=vmem(1)[0],
        cost_estimate=cost(0, 300000),
        compiler_params=params(4),
        name="plane_total",
    )(got)


def enter_kernel(idx_ref, got_ref, planes_ref, out_ref):
    mine = idx_ref[1]
    log = jnp.zeros((8, E), F32)
    low, high = jnp.zeros((8, E), F32), jnp.zeros((8, E), F32)
    for z in range(NZ):
        later = z > mine
        weight = jnp.where(later, jnp.exp(log), 0.0)
        low += weight * planes_ref[z, 0:8, :]
        high += weight * planes_ref[z, 8:16, :]
        log += jnp.where(later, planes_ref[z, ROWS:, :], 0.0)
    for k in range(NP - 1, -1, -1):
        out_ref[k, 0:8, :] = low
        out_ref[k, 8:16, :] = high
        decay = jnp.exp(got_ref[k, ROWS:, :])
        low = got_ref[k, 0:8, :] + decay * low
        high = got_ref[k, 8:16, :] + decay * high


def enter(idx, got, planes):
    return pl.pallas_call(
        enter_kernel,
        out_shape=jax.ShapeDtypeStruct((NP, ROWS, E), F32),
        in_specs=[SMEM] + vmem(2),
        out_specs=vmem(1)[0],
        cost_estimate=cost(0, 400000),
        compiler_params=params(4),
        name="enter",
    )(idx, got, planes)


def weight_kernel(
    idx_ref, state_ref, own_ref, back_ref, k_ref, v_ref, ld_ref, *refs
):
    x_refs, (keep_ref, send_ref, part) = refs[:NH], refs[NH:]
    column, _ = log_sums(ld_ref[...])
    tail = jnp.exp(column[LEN - 1 :, :] - column)
    state = state_ref[...].reshape(E, E)
    high = state.astype(BF16)
    low = (state - high.astype(F32)).astype(BF16)
    k, v = k_ref[...], v_ref[...]
    far_k = mm(v, high, NT) + mm(v, low, NT)
    far_v = mm(k, high, NN) + mm(k, low, NN)
    key_grad = (own_ref[:, :E] + back_ref[:, :E] + tail * far_k).astype(BF16)
    value_grad = (own_ref[:, E:] + back_ref[:, E:] + tail * far_v).astype(BF16)
    grad = jnp.concatenate([key_grad, value_grad], axis=1)
    core, head = idx_ref[2], idx_ref[3]
    for i in range(NH):
        found = mm(x_refs[i][...], grad, TN).reshape(NH, NY, NC, 16, 2 * E)
        for y in range(NY):
            for c in range(NC):
                part[c, y] = found[:, y, c]
        where = pl.ds(lax.rem(head + NH - i, NH) * NH, NH)
        keep_ref[:, where] = part[core]
        send_ref[:, where] = part[1 - core].astype(BF16)


def weight_parts(idx, state, own, back, k, v, ld, xs):
    whole = (NY, NZ, 16, 2 * E)
    return pl.pallas_call(
        weight_kernel,
        out_shape=(jax.ShapeDtypeStruct(whole, F32), jax.ShapeDtypeStruct(whole, BF16)),
        in_specs=[SMEM] + vmem(6 + NH),
        out_specs=tuple(vmem(2)),
        scratch_shapes=[pltpu.VMEM((NC, NY, NH, 16, 2 * E), F32)],
        cost_estimate=cost(2 * NH * XD * LEN * 2 * E, 3500000),
        compiler_params=params(16),
        name="weight_parts",
    )(idx, state, own, back, k, v, ld, *xs)


def merge_kernel(keep_ref, other_ref, out_ref):
    out_ref[...] = (keep_ref[...] + other_ref[...].astype(F32)).astype(BF16)


def merge(keep, other):
    return pl.pallas_call(
        merge_kernel,
        out_shape=jax.ShapeDtypeStruct(other.shape, BF16),
        in_specs=vmem(2),
        out_specs=vmem(1)[0],
        cost_estimate=cost(0, 2000000),
        compiler_params=params(8),
        name="merge",
    )(keep, other)


def fold_kernel(parts_ref, out_ref):
    total = parts_ref[0].astype(F32)
    for y in range(1, NY):
        total += parts_ref[y].astype(F32)
    out_ref[...] = total.astype(BF16)


def fold(parts):
    return pl.pallas_call(
        fold_kernel,
        out_shape=jax.ShapeDtypeStruct(parts.shape[1:], BF16),
        in_specs=vmem(1),
        out_specs=vmem(1)[0],
        cost_estimate=cost(0, 700000),
        compiler_params=params(8),
        name="fold",
    )(parts)


def finish_kernel(parts_ref, key_ref, value_ref):
    total = parts_ref[0].astype(F32)
    for z in range(1, NZ):
        total += parts_ref[z].astype(F32)
    key_ref[...] = total[:, :E].astype(BF16)
    value_ref[...] = total[:, E:].astype(BF16)


def finish(parts):
    shape = jax.ShapeDtypeStruct((16, E), BF16)
    return pl.pallas_call(
        finish_kernel,
        out_shape=(shape, shape),
        in_specs=vmem(1),
        out_specs=tuple(vmem(2)),
        cost_estimate=cost(0, 150000),
        compiler_params=params(4),
        name="finish",
    )(parts)


def shifted(value, steps):
    count = NZ * NP
    leading, last = (max(0, -steps), min(count, count - steps))
    return lax.ppermute(value, CTX, [(source, source + steps) for source in range(leading, last)])


def on_device(layer_input, queries, keys, values, result_cotangent, log_decay):
    axes = (CTX, "z", "core", "head")
    idx = jnp.stack([lax.axis_index(axis) for axis in axes]).astype(jnp.int32)
    got = lax.all_to_all(summary(queries, result_cotangent, log_decay), PLANE, 0, 0, tiled=True)
    prior = shifted(jnp.concatenate([keys, values], axis=1), 1)
    xs = [layer_input] + [
        lax.ppermute(layer_input, "head", [(i, (i + s) % NH) for i in range(NH)])
        for s in range(1, NH)
    ]
    planes = lax.all_to_all(plane_total(got), "z", 0, 0, tiled=True)
    own, old = local(idx, queries, result_cotangent, keys, values, prior, log_decay)
    back = shifted(old, -1)
    state = lax.all_to_all(enter(idx, got, planes), PLANE, 0, 0, tiled=True)
    keep, send = weight_parts(idx, state, own, back, keys, values, log_decay, xs)
    other = lax.ppermute(send, "core", [(0, 1), (1, 0)])
    parts = fold(lax.all_to_all(merge(keep, other), "y", 0, 0, tiled=True))
    return finish(lax.all_to_all(parts, "z", 0, 0, tiled=True))


def solution(mesh):
    fine = Mesh(mesh.devices.reshape(NZ, NY, NC, NH), CTX + ("head",))
    rows = P(CTX, "head")
    in_specs = (rows, rows, rows, rows, rows, P("head", CTX))
    return jax.shard_map(
        on_device, mesh=fine, in_specs=in_specs, out_specs=(rows, rows), check_vma=False
    )
```

```python
import jax
import jax.numpy as jnp
from jax import lax
from jax.experimental import pallas as pl
from jax.experimental.pallas import tpu as pltpu
from jax.sharding import Mesh, PartitionSpec as P


E = 128
LEN = 256
NZ, NY, NC = 16, 4, 2
NP = NY * NC
NH = 4
XD = 512
ROWS = E // NP
LIN = 1.0 / (32 * E)
FACTOR = E ** (-0.5)
F32, BF16 = jnp.float32, jnp.bfloat16

neg_fill = -1e30

PLANE = ("y", "core")
CTX = ("z", "y", "core")

NN = (((1,), (0,)), ((), ()))
NT = (((1,), (1,)), ((), ()))
TN = (((0,), (0,)), ((), ()))


def mm(a, b, dims):
    return lax.dot_general(a, b, dims, preferred_element_type=F32)


def vmem(count):
    return [pl.BlockSpec(memory_space=pltpu.VMEM)] * count


SMEM = pl.BlockSpec(memory_space=pltpu.SMEM)


def cost(flops, nbytes):
    return pl.CostEstimate(flops=flops, bytes_accessed=nbytes, transcendentals=0)


def params(mib):
    return pltpu.CompilerParams(vmem_limit_bytes=mib << 20)


def log_sums(ld):
    t = lax.broadcasted_iota(jnp.int32, (LEN, LEN), 0)
    u = lax.broadcasted_iota(jnp.int32, (LEN, LEN), 1)
    column = jnp.sum(jnp.where(u <= t, ld, 0.0), axis=1, keepdims=True)
    row = jnp.sum(jnp.where(u == t, column, 0.0), axis=0, keepdims=True)
    return column, row


def summary_kernel(q_ref, c_ref, ld_ref, out_ref):
    column, _ = log_sums(ld_ref[...])
    grow = jnp.exp(column)
    total = jnp.zeros((E, E), F32)
    for r in range(2):
        cols = slice(r * E, (r + 1) * E)
        half = c_ref[:, cols].astype(F32) * 0.5
        total += mm(q_ref[:, cols], (grow * half).astype(BF16), TN)
    last = jnp.broadcast_to(column[LEN - 1 :, :], (8, E))
    for m in range(NP):
        out_ref[m, :ROWS, :] = total[m * ROWS : (m + 1) * ROWS] * LIN
        out_ref[m, ROWS:, :] = last


def summary(q, c, ld):
    return pl.pallas_call(
        summary_kernel,
        out_shape=jax.ShapeDtypeStruct((NP, ROWS + 8, E), F32),
        in_specs=vmem(3),
        out_specs=vmem(1)[0],
        cost_estimate=cost(2 * LEN * E * E * 2, 400000),
        compiler_params=params(60),
        name="summary",
    )(q, c, ld)


def local_kernel(idx_ref, q_ref, c_ref, k_ref, v_ref, prior_ref, ld_ref, own_ref, back_ref):
    column, row = log_sums(ld_ref[...])
    j = lax.broadcasted_iota(jnp.int32, (LEN, LEN), 0)
    t = lax.broadcasted_iota(jnp.int32, (LEN, LEN), 1)
    inside = j <= t
    mixing = jnp.exp(jnp.where(inside, row - column, neg_fill))
    outside = jnp.where(idx_ref[0] > 0, 0.0, neg_fill)
    k, v = k_ref[...], v_ref[...]
    prior_k, prior_v = prior_ref[:, :E], prior_ref[:, E:]
    own_k, own_v = jnp.zeros((LEN, E), F32), jnp.zeros((LEN, E), F32)
    win_k, win_v = jnp.zeros((LEN, E), F32), jnp.zeros((LEN, E), F32)
    old_k, old_v = jnp.zeros((LEN, E), F32), jnp.zeros((LEN, E), F32)
    zero = jnp.zeros((LEN, LEN), BF16)
    for r in range(2):
        cols = slice(r * E, (r + 1) * E)
        q = q_ref[:, cols]
        half = (c_ref[:, cols].astype(F32) * 0.5).astype(BF16)
        raw = mm(k, q, NT)
        prod = mm(v, half, NT)
        scores = jnp.where(inside, raw * FACTOR, mm(prior_k, q, NT) * FACTOR + outside)
        dprob = jnp.where(inside, prod, mm(prior_v, half, NT))
        expo = jnp.exp(scores - jnp.max(scores, axis=0, keepdims=True))
        attend = expo / jnp.sum(expo, axis=0, keepdims=True)
        delta = jnp.sum(attend * dprob, axis=0, keepdims=True)
        dscore = (attend * (dprob - delta)).astype(BF16)
        low = attend.astype(BF16)
        own_k += mm((mixing * prod).astype(BF16), q, NN)
        own_v += mm((mixing * raw).astype(BF16), half, NN)
        win_k += mm(jnp.where(inside, dscore, zero), q, NN)
        win_v += mm(jnp.where(inside, low, zero), half, NN)
        old_k += mm(jnp.where(inside, zero, dscore), q, NN)
        old_v += mm(jnp.where(inside, zero, low), half, NN)
    own_ref[:, :E] = own_k * LIN + win_k * FACTOR
    own_ref[:, E:] = own_v * LIN + win_v
    back_ref[:, :E] = old_k * FACTOR
    back_ref[:, E:] = old_v


def local(idx, q, c, k, v, prior, ld):
    shape = jax.ShapeDtypeStruct((LEN, 2 * E), F32)
    return pl.pallas_call(
        local_kernel,
        out_shape=(shape, shape),
        in_specs=[SMEM] + vmem(6),
        out_specs=tuple(vmem(2)),
        cost_estimate=cost(2 * 20 * LEN * LEN * E, 1200000),
        compiler_params=params(16),
        name="local",
    )(idx, q, c, k, v, prior, ld)


def plane_kernel(got_ref, out_ref):
    log = jnp.zeros((8, E), F32)
    low, high = jnp.zeros((8, E), F32), jnp.zeros((8, E), F32)
    for k in range(NP):
        weight = jnp.exp(log)
        low += weight * got_ref[k, 0:8, :]
        high += weight * got_ref[k, 8:16, :]
        log += got_ref[k, ROWS:, :]
    for z in range(NZ):
        out_ref[z, 0:8, :] = low
        out_ref[z, 8:16, :] = high
        out_ref[z, ROWS:, :] = log


def plane_total(got):
    return pl.pallas_call(
        plane_kernel,
        out_shape=jax.ShapeDtypeStruct((NZ, ROWS + 8, E), F32),
        in_specs=vmem(1),
        out_specs=vmem(1)[0],
        cost_estimate=cost(0, 300000),
        compiler_params=params(4),
        name="plane_total",
    )(got)


def enter_kernel(idx_ref, got_ref, planes_ref, out_ref):
    mine = idx_ref[1]
    log = jnp.zeros((8, E), F32)
    low, high = jnp.zeros((8, E), F32), jnp.zeros((8, E), F32)
    for z in range(NZ):
        later = z > mine
        weight = jnp.where(later, jnp.exp(log), 0.0)
        low += weight * planes_ref[z, 0:8, :]
        high += weight * planes_ref[z, 8:16, :]
        log += jnp.where(later, planes_ref[z, ROWS:, :], 0.0)
    for k in range(NP - 1, -1, -1):
        out_ref[k, 0:8, :] = low
        out_ref[k, 8:16, :] = high
        decay = jnp.exp(got_ref[k, ROWS:, :])
        low = got_ref[k, 0:8, :] + decay * low
        high = got_ref[k, 8:16, :] + decay * high


def enter(idx, got, planes):
    return pl.pallas_call(
        enter_kernel,
        out_shape=jax.ShapeDtypeStruct((NP, ROWS, E), F32),
        in_specs=[SMEM] + vmem(2),
        out_specs=vmem(1)[0],
        cost_estimate=cost(0, 400000),
        compiler_params=params(4),
        name="enter",
    )(idx, got, planes)


def weight_kernel(
    idx_ref, state_ref, own_ref, back_ref, k_ref, v_ref, ld_ref, *refs
):
    x_refs, (keep_ref, send_ref, part) = refs[:NH], refs[NH:]
    column, _ = log_sums(ld_ref[...])
    tail = jnp.exp(column[LEN - 1 :, :] - column)
    state = state_ref[...].reshape(E, E)
    high = state.astype(BF16)
    low = (state - high.astype(F32)).astype(BF16)
    k, v = k_ref[...], v_ref[...]
    far_k = mm(v, high, NT) + mm(v, low, NT)
    far_v = mm(k, high, NN) + mm(k, low, NN)
    key_grad = (own_ref[:, :E] + back_ref[:, :E] + tail * far_k).astype(BF16)
    value_grad = (own_ref[:, E:] + back_ref[:, E:] + tail * far_v).astype(BF16)
    grad = jnp.concatenate([key_grad, value_grad], axis=1)
    core, head = idx_ref[2], idx_ref[3]
    for i in range(NH):
        found = mm(x_refs[i][...], grad, TN).reshape(NH, NY, NC, 16, 2 * E)
        for y in range(NY):
            for c in range(NC):
                part[c, y] = found[:, y, c]
        where = pl.ds(lax.rem(head + NH - i, NH) * NH, NH)
        keep_ref[:, where] = part[core]
        send_ref[:, where] = part[1 - core].astype(BF16)


def weight_parts(idx, state, own, back, k, v, ld, xs):
    whole = (NY, NZ, 16, 2 * E)
    return pl.pallas_call(
        weight_kernel,
        out_shape=(jax.ShapeDtypeStruct(whole, F32), jax.ShapeDtypeStruct(whole, BF16)),
        in_specs=[SMEM] + vmem(6 + NH),
        out_specs=tuple(vmem(2)),
        scratch_shapes=[pltpu.VMEM((NC, NY, NH, 16, 2 * E), F32)],
        cost_estimate=cost(2 * NH * XD * LEN * 2 * E, 3500000),
        compiler_params=params(16),
        name="weight_parts",
    )(idx, state, own, back, k, v, ld, *xs)


def merge_kernel(keep_ref, other_ref, out_ref):
    out_ref[...] = (keep_ref[...] + other_ref[...].astype(F32)).astype(BF16)


def merge(keep, other):
    return pl.pallas_call(
        merge_kernel,
        out_shape=jax.ShapeDtypeStruct(other.shape, BF16),
        in_specs=vmem(2),
        out_specs=vmem(1)[0],
        cost_estimate=cost(0, 2000000),
        compiler_params=params(8),
        name="merge",
    )(keep, other)


def fold_kernel(parts_ref, out_ref):
    total = parts_ref[0].astype(F32)
    for y in range(1, NY):
        total += parts_ref[y].astype(F32)
    out_ref[...] = total.astype(BF16)


def fold(parts):
    return pl.pallas_call(
        fold_kernel,
        out_shape=jax.ShapeDtypeStruct(parts.shape[1:], BF16),
        in_specs=vmem(1),
        out_specs=vmem(1)[0],
        cost_estimate=cost(0, 700000),
        compiler_params=params(8),
        name="fold",
    )(parts)


def finish_kernel(parts_ref, key_ref, value_ref):
    total = parts_ref[0].astype(F32)
    for z in range(1, NZ):
        total += parts_ref[z].astype(F32)
    key_ref[...] = total[:, :E].astype(BF16)
    value_ref[...] = total[:, E:].astype(BF16)


def finish(parts):
    shape = jax.ShapeDtypeStruct((16, E), BF16)
    return pl.pallas_call(
        finish_kernel,
        out_shape=(shape, shape),
        in_specs=vmem(1),
        out_specs=tuple(vmem(2)),
        cost_estimate=cost(0, 150000),
        compiler_params=params(4),
        name="finish",
    )(parts)


def shifted(value, steps):
    count = NZ * NP
    leading, last = (max(0, -steps), min(count, count - steps))
    return lax.ppermute(value, CTX, [(source, source + steps) for source in range(leading, last)])


def exchange(value, axis):
    return lax.all_to_all(value, axis, 0, 0, tiled=True)


def on_device(layer_input, queries, keys, values, result_cotangent, log_decay):
    axes = (CTX, "z", "core", "head")
    idx = jnp.stack([lax.axis_index(axis) for axis in axes]).astype(jnp.int32)
    got = exchange(summary(queries, result_cotangent, log_decay), PLANE)
    pair = jnp.concatenate([keys, values], axis=1)
    prior = shifted(pair, 1)
    xs = [layer_input]
    for s in range(1, NH):
        xs.append(lax.ppermute(layer_input, "head", [(i, (i + s) % NH) for i in range(NH)]))
    total = plane_total(got)
    planes = exchange(total, "z")
    own, old = local(idx, queries, result_cotangent, keys, values, prior, log_decay)
    back = shifted(old, -1)
    entering = enter(idx, got, planes)
    state = exchange(entering, PLANE)
    keep, send = weight_parts(idx, state, own, back, keys, values, log_decay, xs)
    other = lax.ppermute(send, "core", [(0, 1), (1, 0)])
    parts = fold(exchange(merge(keep, other), "y"))
    return finish(exchange(parts, "z"))


def solution(mesh):
    fine = Mesh(mesh.devices.reshape(NZ, NY, NC, NH), CTX + ("head",))
    rows = P(CTX, "head")
    in_specs = (rows, rows, rows, rows, rows, P("head", CTX))

    return jax.shard_map(
        on_device, mesh=fine, in_specs=in_specs, out_specs=(rows, rows), check_vma=False
    )
```

```python
import jax
import jax.numpy as jnp
from jax import lax
from jax.experimental import pallas as pl
from jax.experimental.pallas import tpu as pltpu
from jax.sharding import Mesh, PartitionSpec as P


E = 128
LEN = 256
NZ, NY, NC = 16, 4, 2
NP = NY * NC
NH = 4
XD = 512
ROWS = E // NP
LIN = 1.0 / (32 * E)
FACTOR = E ** (-0.5)
F32, BF16 = jnp.float32, jnp.bfloat16

neg_fill = -1e30

PLANE = ("y", "core")
CTX = ("z", "y", "core")

NN = (((1,), (0,)), ((), ()))
NT = (((1,), (1,)), ((), ()))
TN = (((0,), (0,)), ((), ()))


def mm(a, b, dims):
    return lax.dot_general(a, b, dims, preferred_element_type=F32)


def vmem(count):
    return [pl.BlockSpec(memory_space=pltpu.VMEM)] * count


SMEM = pl.BlockSpec(memory_space=pltpu.SMEM)


def cost(flops, nbytes):
    return pl.CostEstimate(flops=flops, bytes_accessed=nbytes, transcendentals=0)


def params(mib):
    return pltpu.CompilerParams(vmem_limit_bytes=mib << 20)


def log_sums(ld):
    t = lax.broadcasted_iota(jnp.int32, (LEN, LEN), 0)
    u = lax.broadcasted_iota(jnp.int32, (LEN, LEN), 1)
    column = jnp.sum(jnp.where(u <= t, ld, 0.0), axis=1, keepdims=True)
    row = jnp.sum(jnp.where(u == t, column, 0.0), axis=0, keepdims=True)
    return column, row


def summary_kernel(q_ref, c_ref, ld_ref, out_ref):
    column, _ = log_sums(ld_ref[...])
    grow = jnp.exp(column)
    total = jnp.zeros((E, E), F32)
    for r in range(2):
        cols = slice(r * E, (r + 1) * E)
        half = c_ref[:, cols].astype(F32) * 0.5
        total += mm(q_ref[:, cols], (grow * half).astype(BF16), TN)
    last = jnp.broadcast_to(column[LEN - 1 :, :], (8, E))
    for m in range(NP):
        out_ref[m, :ROWS, :] = total[m * ROWS : (m + 1) * ROWS] * LIN
        out_ref[m, ROWS:, :] = last


def summary(q, c, ld):
    return pl.pallas_call(
        summary_kernel,
        out_shape=jax.ShapeDtypeStruct((NP, ROWS + 8, E), F32),
        in_specs=vmem(3),
        out_specs=vmem(1)[0],
        cost_estimate=cost(2 * LEN * E * E * 2, 400000),
        compiler_params=params(60),
        name="summary",
    )(q, c, ld)


def pair_kernel(own_ref, got_ref, out_ref):
    out_ref[0] = own_ref[...].T
    out_ref[1] = got_ref[...].T


def pair_up(own, got):
    return pl.pallas_call(
        pair_kernel,
        out_shape=jax.ShapeDtypeStruct((2, XD, LEN), BF16),
        in_specs=vmem(2),
        out_specs=vmem(1)[0],
        cost_estimate=cost(0, 1000000),
        compiler_params=params(8),
        name="pair_up",
    )(own, got)


def local_kernel(idx_ref, q_ref, c_ref, k_ref, v_ref, prior_ref, ld_ref, own_ref, back_ref):
    column, row = log_sums(ld_ref[...])
    j = lax.broadcasted_iota(jnp.int32, (LEN, LEN), 0)
    t = lax.broadcasted_iota(jnp.int32, (LEN, LEN), 1)
    inside = j <= t
    mixing = jnp.exp(jnp.where(inside, row - column, neg_fill))
    outside = jnp.where(idx_ref[0] > 0, 0.0, neg_fill)
    k, v = k_ref[...], v_ref[...]
    prior_k, prior_v = prior_ref[:, :E], prior_ref[:, E:]
    own_k, own_v = jnp.zeros((LEN, E), F32), jnp.zeros((LEN, E), F32)
    win_k, win_v = jnp.zeros((LEN, E), F32), jnp.zeros((LEN, E), F32)
    old_k, old_v = jnp.zeros((LEN, E), F32), jnp.zeros((LEN, E), F32)
    zero = jnp.zeros((LEN, LEN), BF16)
    for r in range(2):
        cols = slice(r * E, (r + 1) * E)
        q = q_ref[:, cols]
        half = (c_ref[:, cols].astype(F32) * 0.5).astype(BF16)
        raw = mm(k, q, NT)
        prod = mm(v, half, NT)
        scores = jnp.where(inside, raw * FACTOR, mm(prior_k, q, NT) * FACTOR + outside)
        dprob = jnp.where(inside, prod, mm(prior_v, half, NT))
        expo = jnp.exp(scores - jnp.max(scores, axis=0, keepdims=True))
        attend = expo / jnp.sum(expo, axis=0, keepdims=True)
        delta = jnp.sum(attend * dprob, axis=0, keepdims=True)
        dscore = (attend * (dprob - delta)).astype(BF16)
        low = attend.astype(BF16)
        own_k += mm((mixing * prod).astype(BF16), q, NN)
        own_v += mm((mixing * raw).astype(BF16), half, NN)
        win_k += mm(jnp.where(inside, dscore, zero), q, NN)
        win_v += mm(jnp.where(inside, low, zero), half, NN)
        old_k += mm(jnp.where(inside, zero, dscore), q, NN)
        old_v += mm(jnp.where(inside, zero, low), half, NN)
    own_ref[:, :E] = own_k * LIN + win_k * FACTOR
    own_ref[:, E:] = own_v * LIN + win_v
    back_ref[:, :E] = old_k * FACTOR
    back_ref[:, E:] = old_v


def local(idx, q, c, k, v, prior, ld):
    shape = jax.ShapeDtypeStruct((LEN, 2 * E), F32)
    return pl.pallas_call(
        local_kernel,
        out_shape=(shape, shape),
        in_specs=[SMEM] + vmem(6),
        out_specs=tuple(vmem(2)),
        cost_estimate=cost(2 * 20 * LEN * LEN * E, 1200000),
        compiler_params=params(16),
        name="local",
    )(idx, q, c, k, v, prior, ld)


def plane_kernel(got_ref, out_ref):
    log = jnp.zeros((8, E), F32)
    low, high = jnp.zeros((8, E), F32), jnp.zeros((8, E), F32)
    for k in range(NP):
        weight = jnp.exp(log)
        low += weight * got_ref[k, 0:8, :]
        high += weight * got_ref[k, 8:16, :]
        log += got_ref[k, ROWS:, :]
    row = lax.broadcasted_iota(jnp.int32, (8, E), 0)
    first = log.astype(BF16).astype(F32)
    second = (log - first).astype(BF16).astype(F32)
    third = log - first - second
    terms = jnp.where(row == 0, first, jnp.where(row == 1, second, jnp.where(row == 2, third, 0.0)))
    sent = jnp.concatenate([low, high, terms], axis=0).astype(BF16)
    for z in range(NZ):
        out_ref[z] = sent


def plane_total(got):
    return pl.pallas_call(
        plane_kernel,
        out_shape=jax.ShapeDtypeStruct((NZ, ROWS + 8, E), BF16),
        in_specs=vmem(1),
        out_specs=vmem(1)[0],
        cost_estimate=cost(0, 300000),
        compiler_params=params(4),
        name="plane_total",
    )(got)


def enter_kernel(idx_ref, got_ref, planes_ref, out_ref):
    mine = idx_ref[1]
    log = jnp.zeros((1, E), F32)
    state = jnp.zeros((ROWS, E), F32)
    for z in range(NZ):
        later = z > mine
        plane = planes_ref[z].astype(F32)
        state += jnp.where(later, jnp.exp(log), 0.0) * plane[:ROWS]
        log += jnp.where(later, jnp.sum(plane[ROWS:], axis=0, keepdims=True), 0.0)
    for k in range(NP - 1, -1, -1):
        out_ref[k] = state
        state = got_ref[k, :ROWS, :] + jnp.exp(got_ref[k, ROWS : ROWS + 1, :]) * state


def enter(idx, got, planes):
    return pl.pallas_call(
        enter_kernel,
        out_shape=jax.ShapeDtypeStruct((NP, ROWS, E), F32),
        in_specs=[SMEM] + vmem(2),
        out_specs=vmem(1)[0],
        cost_estimate=cost(0, 400000),
        compiler_params=params(4),
        name="enter",
    )(idx, got, planes)


def weight_kernel(
    idx_ref, state_ref, own_ref, back_ref, k_ref, v_ref, ld_ref, *refs
):
    near_ref, far_ref, keep_ref, send_ref, part = refs
    column, _ = log_sums(ld_ref[...])
    tail = jnp.exp(column[LEN - 1 :, :] - column)
    state = state_ref[...].reshape(E, E)
    high = state.astype(BF16)
    low = (state - high.astype(F32)).astype(BF16)
    k, v = k_ref[...], v_ref[...]
    far_k = mm(v, high, NT) + mm(v, low, NT)
    far_v = mm(k, high, NN) + mm(k, low, NN)
    key_grad = (own_ref[:, :E] + back_ref[:, :E] + tail * far_k).astype(BF16)
    value_grad = (own_ref[:, E:] + back_ref[:, E:] + tail * far_v).astype(BF16)
    grad = jnp.concatenate([key_grad, value_grad], axis=1)
    core, head = idx_ref[2], idx_ref[3]
    for i in range(NH):
        x = (near_ref if i < 2 else far_ref)[i % 2]
        found = mm(x, grad, NN).reshape(NH, NY, NC, 16, 2 * E)
        for y in range(NY):
            for c in range(NC):
                part[c, y] = found[:, y, c]
        where = pl.ds(lax.bitwise_xor(head, jnp.int32((0, 2, 1, 3)[i])) * NH, NH)
        keep_ref[:, where] = part[core]
        send_ref[:, where] = part[1 - core].astype(BF16)


def weight_parts(idx, state, own, back, k, v, ld, near, far):
    whole = (NY, NZ, 16, 2 * E)
    return pl.pallas_call(
        weight_kernel,
        out_shape=(jax.ShapeDtypeStruct(whole, F32), jax.ShapeDtypeStruct(whole, BF16)),
        in_specs=[SMEM] + vmem(8),
        out_specs=tuple(vmem(2)),
        scratch_shapes=[pltpu.VMEM((NC, NY, NH, 16, 2 * E), F32)],
        cost_estimate=cost(2 * NH * XD * LEN * 2 * E, 3500000),
        compiler_params=params(16),
        name="weight_parts",
    )(idx, state, own, back, k, v, ld, near, far)


def merge_kernel(keep_ref, other_ref, out_ref):
    out_ref[...] = (keep_ref[...] + other_ref[...].astype(F32)).astype(BF16)


def merge(keep, other):
    return pl.pallas_call(
        merge_kernel,
        out_shape=jax.ShapeDtypeStruct(other.shape, BF16),
        in_specs=vmem(2),
        out_specs=vmem(1)[0],
        cost_estimate=cost(0, 2000000),
        compiler_params=params(8),
        name="merge",
    )(keep, other)


def fold_kernel(parts_ref, out_ref):
    total = parts_ref[0].astype(F32)
    for y in range(1, NY):
        total += parts_ref[y].astype(F32)
    out_ref[...] = total.astype(BF16)


def fold(parts):
    return pl.pallas_call(
        fold_kernel,
        out_shape=jax.ShapeDtypeStruct(parts.shape[1:], BF16),
        in_specs=vmem(1),
        out_specs=vmem(1)[0],
        cost_estimate=cost(0, 700000),
        compiler_params=params(8),
        name="fold",
    )(parts)


def finish_kernel(parts_ref, key_ref, value_ref):
    total = parts_ref[0].astype(F32)
    for z in range(1, NZ):
        total += parts_ref[z].astype(F32)
    key_ref[...] = total[:, :E].astype(BF16)
    value_ref[...] = total[:, E:].astype(BF16)


def finish(parts):
    shape = jax.ShapeDtypeStruct((16, E), BF16)
    return pl.pallas_call(
        finish_kernel,
        out_shape=(shape, shape),
        in_specs=vmem(1),
        out_specs=tuple(vmem(2)),
        cost_estimate=cost(0, 150000),
        compiler_params=params(4),
        name="finish",
    )(parts)


def shifted(value, steps):
    count = NZ * NP
    leading, last = (max(0, -steps), min(count, count - steps))
    return lax.ppermute(value, CTX, [(source, source + steps) for source in range(leading, last)])


def exchange(value, axis):
    return lax.all_to_all(value, axis, 0, 0, tiled=True)


def on_device(layer_input, queries, keys, values, result_cotangent, log_decay):
    axes = (CTX, "z", "core", "head")
    idx = jnp.stack([lax.axis_index(axis) for axis in axes]).astype(jnp.int32)
    got = exchange(summary(queries, result_cotangent, log_decay), PLANE)
    pair = jnp.concatenate([keys, values], axis=1)
    prior = shifted(pair, 1)
    opposite = lax.ppermute(layer_input, "head", [(i, i ^ 2) for i in range(NH)])
    near = pair_up(layer_input, opposite)
    far = lax.ppermute(near, "head", [(i, i ^ 1) for i in range(NH)])
    total = plane_total(got)
    planes = exchange(total, "z")
    own, old = local(idx, queries, result_cotangent, keys, values, prior, log_decay)
    back = shifted(old, -1)
    entering = enter(idx, got, planes)
    state = exchange(entering, PLANE)
    keep, send = weight_parts(idx, state, own, back, keys, values, log_decay, near, far)
    other = lax.ppermute(send, "core", [(0, 1), (1, 0)])
    parts = fold(exchange(merge(keep, other), "y"))
    return finish(exchange(parts, "z"))


def solution(mesh):
    fine = Mesh(mesh.devices.reshape(NZ, NY, NC, NH), CTX + ("head",))
    rows = P(CTX, "head")
    in_specs = (rows, rows, rows, rows, rows, P("head", CTX))

    return jax.shard_map(
        on_device, mesh=fine, in_specs=in_specs, out_specs=(rows, rows), check_vma=False
    )
```

```python
import jax
import jax.numpy as jnp
from jax import lax
from jax.experimental import pallas as pl
from jax.experimental.pallas import tpu as pltpu
from jax.sharding import Mesh, PartitionSpec as P


E = 128
LEN = 256
NZ, NY, NC = 16, 4, 2
NP = NY * NC
NH = 4
XD = 512
ROWS = E // NP
LIN = 1.0 / (32 * E)
FACTOR = E ** (-0.5)
F32, BF16 = jnp.float32, jnp.bfloat16

neg_fill = -1e30

PLANE = ("y", "core")
CTX = ("z", "y", "core")

NN = (((1,), (0,)), ((), ()))
NT = (((1,), (1,)), ((), ()))
TN = (((0,), (0,)), ((), ()))


def mm(a, b, dims):
    return lax.dot_general(a, b, dims, preferred_element_type=F32)


def vmem(count):
    return [pl.BlockSpec(memory_space=pltpu.VMEM)] * count


SMEM = pl.BlockSpec(memory_space=pltpu.SMEM)


def cost(flops, nbytes):
    return pl.CostEstimate(flops=flops, bytes_accessed=nbytes, transcendentals=0)


def params(mib):
    return pltpu.CompilerParams(vmem_limit_bytes=mib << 20)


def log_sums(ld):
    t = lax.broadcasted_iota(jnp.int32, (LEN, LEN), 0)
    u = lax.broadcasted_iota(jnp.int32, (LEN, LEN), 1)
    column = jnp.sum(jnp.where(u <= t, ld, 0.0), axis=1, keepdims=True)
    row = jnp.sum(jnp.where(u == t, column, 0.0), axis=0, keepdims=True)
    return column, row


def summary_kernel(q_ref, c_ref, ld_ref, out_ref):
    column, _ = log_sums(ld_ref[...])
    grow = jnp.exp(column)
    total = jnp.zeros((E, E), F32)
    for r in range(2):
        cols = slice(r * E, (r + 1) * E)
        half = c_ref[:, cols].astype(F32) * 0.5
        total += mm(q_ref[:, cols], (grow * half).astype(BF16), TN)
    last = jnp.broadcast_to(column[LEN - 1 :, :], (8, E))
    for m in range(NP):
        out_ref[m, :ROWS, :] = total[m * ROWS : (m + 1) * ROWS] * LIN
        out_ref[m, ROWS:, :] = last


def summary(q, c, ld):
    return pl.pallas_call(
        summary_kernel,
        out_shape=jax.ShapeDtypeStruct((NP, ROWS + 8, E), F32),
        in_specs=vmem(3),
        out_specs=vmem(1)[0],
        cost_estimate=cost(2 * LEN * E * E * 2, 400000),
        compiler_params=params(60),
        name="summary",
    )(q, c, ld)


def pair_kernel(own_ref, got_ref, ld_ref, out_ref):
    for i, ref in enumerate((own_ref, got_ref)):
        rows = ref[...].T.reshape(NH * NY, NC, 16, LEN)
        for core in range(NC):
            out_ref[i, core] = rows[:, core].reshape(XD // NC, LEN)


def pair_up(own, got, ld):
    return pl.pallas_call(
        pair_kernel,
        out_shape=jax.ShapeDtypeStruct((2, NC, XD // NC, LEN), BF16),
        in_specs=vmem(3),
        out_specs=vmem(1)[0],
        cost_estimate=cost(0, 1000000),
        compiler_params=params(8),
        name="pair_up",
    )(own, got, ld)


def local_kernel(idx_ref, q_ref, c_ref, k_ref, v_ref, prior_ref, ld_ref, own_ref, back_ref, tail_ref):
    column, row = log_sums(ld_ref[...])
    j = lax.broadcasted_iota(jnp.int32, (LEN, LEN), 0)
    t = lax.broadcasted_iota(jnp.int32, (LEN, LEN), 1)
    inside = j <= t
    mixing = jnp.exp(jnp.where(inside, row - column, neg_fill))
    outside = jnp.where(idx_ref[0] > 0, 0.0, neg_fill)
    k, v = k_ref[...], v_ref[...]
    prior_k, prior_v = prior_ref[:, :E], prior_ref[:, E:]
    own_k, own_v = jnp.zeros((LEN, E), F32), jnp.zeros((LEN, E), F32)
    win_k, win_v = jnp.zeros((LEN, E), F32), jnp.zeros((LEN, E), F32)
    old_k, old_v = jnp.zeros((LEN, E), F32), jnp.zeros((LEN, E), F32)
    zero = jnp.zeros((LEN, LEN), BF16)
    for r in range(2):
        cols = slice(r * E, (r + 1) * E)
        q = q_ref[:, cols]
        half = (c_ref[:, cols].astype(F32) * 0.5).astype(BF16)
        raw = mm(k, q, NT)
        prod = mm(v, half, NT)
        scores = jnp.where(inside, raw * FACTOR, mm(prior_k, q, NT) * FACTOR + outside)
        dprob = jnp.where(inside, prod, mm(prior_v, half, NT))
        expo = jnp.exp(scores - jnp.max(scores, axis=0, keepdims=True))
        attend = expo / jnp.sum(expo, axis=0, keepdims=True)
        delta = jnp.sum(attend * dprob, axis=0, keepdims=True)
        dscore = (attend * (dprob - delta)).astype(BF16)
        low = attend.astype(BF16)
        own_k += mm((mixing * prod).astype(BF16), q, NN)
        own_v += mm((mixing * raw).astype(BF16), half, NN)
        win_k += mm(jnp.where(inside, dscore, zero), q, NN)
        win_v += mm(jnp.where(inside, low, zero), half, NN)
        old_k += mm(jnp.where(inside, zero, dscore), q, NN)
        old_v += mm(jnp.where(inside, zero, low), half, NN)
    own_ref[:, :E] = own_k * LIN + win_k * FACTOR
    own_ref[:, E:] = own_v * LIN + win_v
    back_ref[:, :E] = old_k * FACTOR
    back_ref[:, E:] = old_v
    tail_ref[...] = jnp.broadcast_to(jnp.exp(column[LEN - 1 :, :] - column), (LEN, E))


def local(idx, q, c, k, v, prior, ld):
    shape = jax.ShapeDtypeStruct((LEN, 2 * E), F32)
    return pl.pallas_call(
        local_kernel,
        out_shape=(shape, shape, jax.ShapeDtypeStruct((LEN, E), F32)),
        in_specs=[SMEM] + vmem(6),
        out_specs=tuple(vmem(3)),
        cost_estimate=cost(2 * 20 * LEN * LEN * E, 1200000),
        compiler_params=params(16),
        name="local",
    )(idx, q, c, k, v, prior, ld)


def plane_kernel(got_ref, out_ref):
    log = jnp.zeros((8, E), F32)
    low, high = jnp.zeros((8, E), F32), jnp.zeros((8, E), F32)
    for k in range(NP):
        weight = jnp.exp(log)
        low += weight * got_ref[k, 0:8, :]
        high += weight * got_ref[k, 8:16, :]
        log += got_ref[k, ROWS:, :]
    row = lax.broadcasted_iota(jnp.int32, (8, E), 0)
    first = log.astype(BF16).astype(F32)
    second = (log - first).astype(BF16).astype(F32)
    third = log - first - second
    terms = jnp.where(row == 0, first, jnp.where(row == 1, second, jnp.where(row == 2, third, 0.0)))
    sent = jnp.concatenate([low, high, terms], axis=0).astype(BF16)
    for z in range(NZ):
        out_ref[z] = sent


def plane_total(got):
    return pl.pallas_call(
        plane_kernel,
        out_shape=jax.ShapeDtypeStruct((NZ, ROWS + 8, E), BF16),
        in_specs=vmem(1),
        out_specs=vmem(1)[0],
        cost_estimate=cost(0, 300000),
        compiler_params=params(4),
        name="plane_total",
    )(got)


def enter_kernel(idx_ref, got_ref, planes_ref, out_ref):
    mine = idx_ref[1]
    log = jnp.zeros((1, E), F32)
    state = jnp.zeros((ROWS, E), F32)
    for z in range(NZ):
        later = z > mine
        plane = planes_ref[z].astype(F32)
        state += jnp.where(later, jnp.exp(log), 0.0) * plane[:ROWS]
        log += jnp.where(later, jnp.sum(plane[ROWS:], axis=0, keepdims=True), 0.0)
    for k in range(NP - 1, -1, -1):
        out_ref[k] = state
        state = got_ref[k, :ROWS, :] + jnp.exp(got_ref[k, ROWS : ROWS + 1, :]) * state


def enter(idx, got, planes):
    return pl.pallas_call(
        enter_kernel,
        out_shape=jax.ShapeDtypeStruct((NP, ROWS, E), F32),
        in_specs=[SMEM] + vmem(2),
        out_specs=vmem(1)[0],
        cost_estimate=cost(0, 400000),
        compiler_params=params(4),
        name="enter",
    )(idx, got, planes)


def head_rows(head, i):
    return pl.ds(lax.bitwise_xor(head, jnp.int32((0, 2, 1, 3)[i])) * NH, NH)


def half_weights(near_ref, far_ref, grad, core, head, write):
    for i in range(NH):
        x = (near_ref if i < 2 else far_ref)[i % 2, core]
        found = mm(x, grad, NN).reshape(NH, NY, 16, 2 * E)
        for y in range(NY):
            write(y, head_rows(head, i), found[:, y])


def send_kernel(
    idx_ref, state_ref, own_ref, back_ref, k_ref, v_ref, tail_ref, near_ref, far_ref, send_ref, grad_ref
):
    state = state_ref[...].reshape(E, E)
    high = state.astype(BF16)
    low = (state - high.astype(F32)).astype(BF16)
    k, v, tail = k_ref[...], v_ref[...], tail_ref[...]
    far_k = mm(v, high, NT) + mm(v, low, NT)
    far_v = mm(k, high, NN) + mm(k, low, NN)
    grad_ref[:, :E] = (own_ref[:, :E] + back_ref[:, :E] + tail * far_k).astype(BF16)
    grad_ref[:, E:] = (own_ref[:, E:] + back_ref[:, E:] + tail * far_v).astype(BF16)

    def write(y, where, rows):
        send_ref[y, where] = rows.astype(BF16)

    half_weights(near_ref, far_ref, grad_ref[...], 1 - idx_ref[2], idx_ref[3], write)


WHOLE = (NY, NZ, 16, 2 * E)


def send_half(idx, *operands):
    return pl.pallas_call(
        send_kernel,
        out_shape=(
            jax.ShapeDtypeStruct(WHOLE, BF16),
            jax.ShapeDtypeStruct((LEN, 2 * E), BF16),
        ),
        in_specs=[SMEM] + vmem(8),
        out_specs=tuple(vmem(2)),
        cost_estimate=cost(NH * XD * LEN * 2 * E, 2500000),
        compiler_params=params(16),
        name="send_half",
    )(idx, *operands)


def keep_kernel(idx_ref, grad_ref, near_ref, far_ref, keep_ref):
    def write(y, where, rows):
        keep_ref[y, where] = rows

    half_weights(near_ref, far_ref, grad_ref[...], idx_ref[2], idx_ref[3], write)


def keep_half(idx, *operands):
    return pl.pallas_call(
        keep_kernel,
        out_shape=jax.ShapeDtypeStruct(WHOLE, F32),
        in_specs=[SMEM] + vmem(3),
        out_specs=vmem(1)[0],
        cost_estimate=cost(NH * XD * LEN * 2 * E, 2500000),
        compiler_params=params(16),
        name="keep_half",
    )(idx, *operands)


def shifted(value, steps):
    count = NZ * NP
    leading, last = (max(0, -steps), min(count, count - steps))
    return lax.ppermute(value, CTX, [(source, source + steps) for source in range(leading, last)])


def merge_kernel(keep_ref, other_ref, out_ref):
    out_ref[...] = (keep_ref[...] + other_ref[...].astype(F32)).astype(BF16)


def merge(keep, other):
    return pl.pallas_call(
        merge_kernel,
        out_shape=jax.ShapeDtypeStruct(other.shape, BF16),
        in_specs=vmem(2),
        out_specs=vmem(1)[0],
        cost_estimate=cost(0, 2000000),
        compiler_params=params(8),
        name="merge",
    )(keep, other)


def fold_kernel(parts_ref, out_ref):
    total = parts_ref[0].astype(F32)
    for y in range(1, NY):
        total += parts_ref[y].astype(F32)
    out_ref[...] = total.astype(BF16)


def fold(parts):
    return pl.pallas_call(
        fold_kernel,
        out_shape=jax.ShapeDtypeStruct(parts.shape[1:], BF16),
        in_specs=vmem(1),
        out_specs=vmem(1)[0],
        cost_estimate=cost(0, 700000),
        compiler_params=params(8),
        name="fold",
    )(parts)


def finish_kernel(parts_ref, key_ref, value_ref):
    total = parts_ref[0].astype(F32)
    for z in range(1, NZ):
        total += parts_ref[z].astype(F32)
    key_ref[...] = total[:, :E].astype(BF16)
    value_ref[...] = total[:, E:].astype(BF16)


def finish(parts):
    shape = jax.ShapeDtypeStruct((16, E), BF16)
    return pl.pallas_call(
        finish_kernel,
        out_shape=(shape, shape),
        in_specs=vmem(1),
        out_specs=tuple(vmem(2)),
        cost_estimate=cost(0, 150000),
        compiler_params=params(4),
        name="finish",
    )(parts)


def exchange(value, axis):
    return lax.all_to_all(value, axis, 0, 0, tiled=True)


def on_device(layer_input, queries, keys, values, result_cotangent, log_decay):
    axes = (CTX, "z", "core", "head")
    idx = jnp.stack([lax.axis_index(axis) for axis in axes]).astype(jnp.int32)
    sent = summary(queries, result_cotangent, log_decay)
    got = exchange(sent, PLANE)
    pair = jnp.concatenate([keys, values], axis=1)
    prior = shifted(pair, 1)
    opposite = lax.ppermute(layer_input, "head", [(i, i ^ 2) for i in range(NH)])
    near = pair_up(layer_input, opposite, log_decay)
    far = lax.ppermute(near, "head", [(i, i ^ 1) for i in range(NH)])
    total = plane_total(got)
    planes = exchange(total, "z")
    own, old, tail = local(idx, queries, result_cotangent, keys, values, prior, log_decay)
    back = shifted(old, -1)
    entering = enter(idx, got, planes)
    state = exchange(entering, PLANE)
    send, grad = send_half(idx, state, own, back, keys, values, tail, near, far)
    other = lax.ppermute(send, "core", [(0, 1), (1, 0)])
    keep = keep_half(idx, grad, near, far)
    parts = fold(exchange(merge(keep, other), "y"))
    return finish(exchange(parts, "z"))


def solution(mesh):
    fine = Mesh(mesh.devices.reshape(NZ, NY, NC, NH), CTX + ("head",))
    rows = P(CTX, "head")
    in_specs = (rows, rows, rows, rows, rows, P("head", CTX))

    return jax.shard_map(
        on_device, mesh=fine, in_specs=in_specs, out_specs=(rows, rows), check_vma=False
    )
```

```python
import jax
import jax.numpy as jnp
from jax import lax
from jax.experimental import pallas as pl
from jax.experimental.pallas import tpu as pltpu
from jax.sharding import PartitionSpec as P


E = 128
LEN = 256
NA, NB, NY, NC = 8, 2, 4, 2
NZ = NA * NB
NP = NY * NC
NH = 4
XD = 512
ROWS = E // NP
LIN = 1.0 / (32 * E)
FACTOR = E ** (-0.5)
F32, BF16 = jnp.float32, jnp.bfloat16

neg_fill = -1e30


FIRST, ACROSS, LAST, NEAR, FAR = 7, 10, 0, 7, 4


def place(z, y, core):
    return (z * NY + y) * NC + core


def plane_groups(lead):
    return [[z * NP + (q ^ lead) for q in range(NP)] for z in range(NZ)]


def z_groups(lead):
    return [[(q ^ lead) * NP + p for q in range(NZ)] for p in range(NP)]


def near_groups(lead):
    members = [(q ^ lead) for q in range(NB * NY)]
    return [
        [place(a * NB + m // NY, m % NY, core) for m in members]
        for a in range(NA)
        for core in range(NC)
    ]


def far_groups(lead):
    return [
        [place((q ^ lead) * NB + b, y, core) for q in range(NA)]
        for b in range(NB)
        for y in range(NY)
        for core in range(NC)
    ]


NN = (((1,), (0,)), ((), ()))
NT = (((1,), (1,)), ((), ()))
TN = (((0,), (0,)), ((), ()))


def mm(a, b, dims):
    return lax.dot_general(a, b, dims, preferred_element_type=F32)


def vmem(count):
    return [pl.BlockSpec(memory_space=pltpu.VMEM)] * count


SMEM = pl.BlockSpec(memory_space=pltpu.SMEM)


def cost(flops, nbytes):
    return pl.CostEstimate(flops=flops, bytes_accessed=nbytes, transcendentals=0)


def params(mib):
    return pltpu.CompilerParams(vmem_limit_bytes=mib << 20)


def log_sums(ld):
    t = lax.broadcasted_iota(jnp.int32, (LEN, LEN), 0)
    u = lax.broadcasted_iota(jnp.int32, (LEN, LEN), 1)
    column = jnp.sum(jnp.where(u <= t, ld, 0.0), axis=1, keepdims=True)
    row = jnp.sum(jnp.where(u == t, column, 0.0), axis=0, keepdims=True)
    return column, row


def summary_kernel(q_ref, c_ref, ld_ref, out_ref):
    column, _ = log_sums(ld_ref[...])
    grow = jnp.exp(column)
    total = jnp.zeros((E, E), F32)
    for r in range(2):
        cols = slice(r * E, (r + 1) * E)
        half = c_ref[:, cols].astype(F32) * 0.5
        total += mm(q_ref[:, cols], (grow * half).astype(BF16), TN)
    last = jnp.broadcast_to(column[LEN - 1 :, :], (8, E))
    for m in range(NP):
        out_ref[m ^ FIRST, :ROWS, :] = total[m * ROWS : (m + 1) * ROWS] * LIN
        out_ref[m ^ FIRST, ROWS:, :] = last


def summary(q, c, ld):
    return pl.pallas_call(
        summary_kernel,
        out_shape=jax.ShapeDtypeStruct((NP, ROWS + 8, E), F32),
        in_specs=vmem(3),
        out_specs=vmem(1)[0],
        cost_estimate=cost(2 * LEN * E * E * 2, 400000),
        compiler_params=params(60),
        name="summary",
    )(q, c, ld)


def pair_kernel(own_ref, got_ref, ld_ref, out_ref):
    for i, ref in enumerate((own_ref, got_ref)):
        rows = ref[...].T.reshape(NH * NY, NC, 16, LEN)
        for core in range(NC):
            out_ref[i, core] = rows[:, core].reshape(XD // NC, LEN)


def pair_up(own, got, ld):
    return pl.pallas_call(
        pair_kernel,
        out_shape=jax.ShapeDtypeStruct((2, NC, XD // NC, LEN), BF16),
        in_specs=vmem(3),
        out_specs=vmem(1)[0],
        cost_estimate=cost(0, 1000000),
        compiler_params=params(8),
        name="pair_up",
    )(own, got, ld)


def local_kernel(idx_ref, q_ref, c_ref, k_ref, v_ref, prior_ref, ld_ref, own_ref, back_ref, tail_ref):
    column, row = log_sums(ld_ref[...])
    j = lax.broadcasted_iota(jnp.int32, (LEN, LEN), 0)
    t = lax.broadcasted_iota(jnp.int32, (LEN, LEN), 1)
    inside = j <= t
    mixing = jnp.exp(jnp.where(inside, row - column, neg_fill))
    outside = jnp.where(idx_ref[0] > 0, 0.0, neg_fill)
    k, v = k_ref[...], v_ref[...]
    prior_k, prior_v = prior_ref[:, :E], prior_ref[:, E:]
    own_k, own_v = jnp.zeros((LEN, E), F32), jnp.zeros((LEN, E), F32)
    win_k, win_v = jnp.zeros((LEN, E), F32), jnp.zeros((LEN, E), F32)
    old_k, old_v = jnp.zeros((LEN, E), F32), jnp.zeros((LEN, E), F32)
    zero = jnp.zeros((LEN, LEN), BF16)
    for r in range(2):
        cols = slice(r * E, (r + 1) * E)
        q = q_ref[:, cols]
        half = (c_ref[:, cols].astype(F32) * 0.5).astype(BF16)
        raw = mm(k, q, NT)
        prod = mm(v, half, NT)
        scores = jnp.where(inside, raw * FACTOR, mm(prior_k, q, NT) * FACTOR + outside)
        dprob = jnp.where(inside, prod, mm(prior_v, half, NT))
        expo = jnp.exp(scores - jnp.max(scores, axis=0, keepdims=True))
        attend = expo / jnp.sum(expo, axis=0, keepdims=True)
        delta = jnp.sum(attend * dprob, axis=0, keepdims=True)
        dscore = (attend * (dprob - delta)).astype(BF16)
        low = attend.astype(BF16)
        own_k += mm((mixing * prod).astype(BF16), q, NN)
        own_v += mm((mixing * raw).astype(BF16), half, NN)
        win_k += mm(jnp.where(inside, dscore, zero), q, NN)
        win_v += mm(jnp.where(inside, low, zero), half, NN)
        old_k += mm(jnp.where(inside, zero, dscore), q, NN)
        old_v += mm(jnp.where(inside, zero, low), half, NN)
    own_ref[:, :E] = own_k * LIN + win_k * FACTOR
    own_ref[:, E:] = own_v * LIN + win_v
    back_ref[:, :E] = old_k * FACTOR
    back_ref[:, E:] = old_v
    tail_ref[...] = jnp.broadcast_to(jnp.exp(column[LEN - 1 :, :] - column), (LEN, E))


def local(idx, q, c, k, v, prior, ld):
    shape = jax.ShapeDtypeStruct((LEN, 2 * E), F32)
    return pl.pallas_call(
        local_kernel,
        out_shape=(shape, shape, jax.ShapeDtypeStruct((LEN, E), F32)),
        in_specs=[SMEM] + vmem(6),
        out_specs=tuple(vmem(3)),
        cost_estimate=cost(2 * 20 * LEN * LEN * E, 1200000),
        compiler_params=params(16),
        name="local",
    )(idx, q, c, k, v, prior, ld)


def plane_kernel(got_ref, out_ref):
    log = jnp.zeros((8, E), F32)
    low, high = jnp.zeros((8, E), F32), jnp.zeros((8, E), F32)
    for k in range(NP):
        weight = jnp.exp(log)
        low += weight * got_ref[k ^ FIRST, 0:8, :]
        high += weight * got_ref[k ^ FIRST, 8:16, :]
        log += got_ref[k ^ FIRST, ROWS:, :]
    row = lax.broadcasted_iota(jnp.int32, (8, E), 0)
    first = log.astype(BF16).astype(F32)
    second = (log - first).astype(BF16).astype(F32)
    third = log - first - second
    terms = jnp.where(row == 0, first, jnp.where(row == 1, second, jnp.where(row == 2, third, 0.0)))
    sent = jnp.concatenate([low, high, terms], axis=0).astype(BF16)
    for z in range(NZ):
        out_ref[z] = sent


def plane_total(got):
    return pl.pallas_call(
        plane_kernel,
        out_shape=jax.ShapeDtypeStruct((NZ, ROWS + 8, E), BF16),
        in_specs=vmem(1),
        out_specs=vmem(1)[0],
        cost_estimate=cost(0, 300000),
        compiler_params=params(4),
        name="plane_total",
    )(got)


def enter_kernel(idx_ref, got_ref, planes_ref, out_ref):
    mine = lax.div(idx_ref[0], jnp.int32(NP))
    log = jnp.zeros((1, E), F32)
    state = jnp.zeros((ROWS, E), F32)
    for z in range(NZ):
        later = z > mine
        plane = planes_ref[z ^ ACROSS].astype(F32)
        state += jnp.where(later, jnp.exp(log), 0.0) * plane[:ROWS]
        log += jnp.where(later, jnp.sum(plane[ROWS:], axis=0, keepdims=True), 0.0)
    for k in range(NP - 1, -1, -1):
        out_ref[k ^ LAST] = state
        block = got_ref[k ^ FIRST]
        state = block[:ROWS] + jnp.exp(block[ROWS : ROWS + 1]) * state


def enter(idx, got, planes):
    return pl.pallas_call(
        enter_kernel,
        out_shape=jax.ShapeDtypeStruct((NP, ROWS, E), F32),
        in_specs=[SMEM] + vmem(2),
        out_specs=vmem(1)[0],
        cost_estimate=cost(0, 400000),
        compiler_params=params(4),
        name="enter",
    )(idx, got, planes)


def half_weights(near_ref, far_ref, grad, core, head, write):
    for i in range(NH):
        x = (near_ref if i < 2 else far_ref)[i % 2, core]
        found = mm(x, grad, NN).reshape(NH // NB, NB, NY, 16, 2 * E)
        shard = lax.bitwise_xor(head, jnp.int32((0, 2, 1, 3)[i]))
        count = NH // NB
        where = pl.ds(lax.bitwise_xor(shard, jnp.int32(FAR // count)) * count, count)
        for b in range(NB):
            for y in range(NY):
                write((b * NY + y) ^ NEAR, where, found[:, b, y])


def send_kernel(
    idx_ref, state_ref, own_ref, back_ref, k_ref, v_ref, tail_ref, near_ref, far_ref, send_ref, grad_ref
):
    state = jnp.concatenate([state_ref[m ^ LAST] for m in range(NP)], axis=0)
    high = state.astype(BF16)
    low = (state - high.astype(F32)).astype(BF16)
    k, v, tail = k_ref[...], v_ref[...], tail_ref[...]
    far_k = mm(v, high, NT) + mm(v, low, NT)
    far_v = mm(k, high, NN) + mm(k, low, NN)
    grad_ref[:, :E] = (own_ref[:, :E] + back_ref[:, :E] + tail * far_k).astype(BF16)
    grad_ref[:, E:] = (own_ref[:, E:] + back_ref[:, E:] + tail * far_v).astype(BF16)

    def write(near, where, rows):
        send_ref[near, where] = rows.astype(BF16)

    half_weights(near_ref, far_ref, grad_ref[...], 1 - lax.rem(idx_ref[0], jnp.int32(NC)), idx_ref[1], write)


WHOLE = (NB * NY, NA, 16, 2 * E)


def send_half(idx, *operands):
    return pl.pallas_call(
        send_kernel,
        out_shape=(
            jax.ShapeDtypeStruct(WHOLE, BF16),
            jax.ShapeDtypeStruct((LEN, 2 * E), BF16),
        ),
        in_specs=[SMEM] + vmem(8),
        out_specs=tuple(vmem(2)),
        cost_estimate=cost(NH * XD * LEN * 2 * E, 2500000),
        compiler_params=params(16),
        name="send_half",
    )(idx, *operands)


def keep_kernel(idx_ref, grad_ref, near_ref, far_ref, keep_ref):
    def write(near, where, rows):
        keep_ref[near, where] = rows

    half_weights(near_ref, far_ref, grad_ref[...], lax.rem(idx_ref[0], jnp.int32(NC)), idx_ref[1], write)


def keep_half(idx, *operands):
    return pl.pallas_call(
        keep_kernel,
        out_shape=jax.ShapeDtypeStruct(WHOLE, F32),
        in_specs=[SMEM] + vmem(3),
        out_specs=vmem(1)[0],
        cost_estimate=cost(NH * XD * LEN * 2 * E, 2500000),
        compiler_params=params(16),
        name="keep_half",
    )(idx, *operands)


def shifted(value, steps):
    count = NZ * NP
    leading, last = (max(0, -steps), min(count, count - steps))
    return lax.ppermute(value, "ctx", [(source, source + steps) for source in range(leading, last)])


def merge_kernel(keep_ref, other_ref, out_ref):
    out_ref[...] = (keep_ref[...] + other_ref[...].astype(F32)).astype(BF16)


def merge(keep, other):
    return pl.pallas_call(
        merge_kernel,
        out_shape=jax.ShapeDtypeStruct(other.shape, BF16),
        in_specs=vmem(2),
        out_specs=vmem(1)[0],
        cost_estimate=cost(0, 2000000),
        compiler_params=params(8),
        name="merge",
    )(keep, other)


def summed(parts_ref):
    total = parts_ref[0].astype(F32)
    for i in range(1, parts_ref.shape[0]):
        total += parts_ref[i].astype(F32)
    return total


def fold_kernel(parts_ref, out_ref):
    out_ref[...] = summed(parts_ref).astype(BF16)


def fold(parts):
    return pl.pallas_call(
        fold_kernel,
        out_shape=jax.ShapeDtypeStruct(parts.shape[1:], BF16),
        in_specs=vmem(1),
        out_specs=vmem(1)[0],
        cost_estimate=cost(0, 600000),
        compiler_params=params(8),
        name="fold",
    )(parts)


def finish_kernel(parts_ref, key_ref, value_ref):
    total = summed(parts_ref)
    key_ref[...] = total[:, :E].astype(BF16)
    value_ref[...] = total[:, E:].astype(BF16)


def finish(parts):
    shape = jax.ShapeDtypeStruct((16, E), BF16)
    return pl.pallas_call(
        finish_kernel,
        out_shape=(shape, shape),
        in_specs=vmem(1),
        out_specs=tuple(vmem(2)),
        cost_estimate=cost(0, 150000),
        compiler_params=params(4),
        name="finish",
    )(parts)


def exchange(value, groups):
    return lax.all_to_all(value, "ctx", 0, 0, axis_index_groups=groups, tiled=True)


def on_device(layer_input, queries, keys, values, result_cotangent, log_decay):
    idx = jnp.stack([lax.axis_index("ctx"), lax.axis_index("head")]).astype(jnp.int32)
    sent = summary(queries, result_cotangent, log_decay)
    got = exchange(sent, plane_groups(FIRST))
    pair = jnp.concatenate([keys, values], axis=1)
    prior = shifted(pair, 1)
    opposite = lax.ppermute(layer_input, "head", [(i, i ^ 2) for i in range(NH)])
    near = pair_up(layer_input, opposite, log_decay)
    far = lax.ppermute(near, "head", [(i, i ^ 1) for i in range(NH)])
    total = plane_total(got)
    planes = exchange(total, z_groups(ACROSS))
    own, old, tail = local(idx, queries, result_cotangent, keys, values, prior, log_decay)
    back = shifted(old, -1)
    entering = enter(idx, got, planes)
    state = exchange(entering, plane_groups(LAST))
    send, grad = send_half(idx, state, own, back, keys, values, tail, near, far)
    other = lax.ppermute(send, "ctx", [(i, i ^ 1) for i in range(NZ * NP)])
    keep = keep_half(idx, grad, near, far)
    parts = fold(exchange(merge(keep, other), near_groups(NEAR)))
    return finish(exchange(parts, far_groups(FAR)))


def solution(mesh):
    rows = P("ctx", "head")
    in_specs = (rows, rows, rows, rows, rows, P("head", "ctx"))

    return jax.shard_map(
        on_device, mesh=mesh, in_specs=in_specs, out_specs=(rows, rows), check_vma=False
    )
```

```python
import jax
import jax.numpy as jnp
from jax import lax
from jax.experimental import pallas as pl
from jax.experimental.pallas import tpu as pltpu
from jax.sharding import PartitionSpec as P


E = 128
LEN = 256
NA, NB, NY, NC = 8, 2, 4, 2
NZ = NA * NB
NP = NY * NC
NH = 4
XD = 512
ROWS = E // NP
LIN = 1.0 / (32 * E)
FACTOR = E ** (-0.5)
F32, BF16 = jnp.float32, jnp.bfloat16

neg_fill = -1e30


FIRST, ACROSS, LAST, NEAR, FAR = 7, 10, 2, 6, 4


def place(z, y, core):
    return (z * NY + y) * NC + core


def plane_groups(lead):
    return [[z * NP + (q ^ lead) for q in range(NP)] for z in range(NZ)]


def z_groups(lead):
    return [[(q ^ lead) * NP + p for q in range(NZ)] for p in range(NP)]


def near_groups(lead):
    members = [(q ^ lead) for q in range(NB * NY)]
    return [
        [place(a * NB + m // NY, m % NY, core) for m in members]
        for a in range(NA)
        for core in range(NC)
    ]


def far_groups(lead):
    return [
        [place((q ^ lead) * NB + b, y, core) for q in range(NA)]
        for b in range(NB)
        for y in range(NY)
        for core in range(NC)
    ]


NN = (((1,), (0,)), ((), ()))
NT = (((1,), (1,)), ((), ()))
TN = (((0,), (0,)), ((), ()))


def mm(a, b, dims):
    return lax.dot_general(a, b, dims, preferred_element_type=F32)


def vmem(count):
    return [pl.BlockSpec(memory_space=pltpu.VMEM)] * count


SMEM = pl.BlockSpec(memory_space=pltpu.SMEM)


def cost(flops, nbytes):
    return pl.CostEstimate(flops=flops, bytes_accessed=nbytes, transcendentals=0)


def params(mib):
    return pltpu.CompilerParams(vmem_limit_bytes=mib << 20)


def log_sums(ld):
    t = lax.broadcasted_iota(jnp.int32, (LEN, LEN), 0)
    u = lax.broadcasted_iota(jnp.int32, (LEN, LEN), 1)
    column = jnp.sum(jnp.where(u <= t, ld, 0.0), axis=1, keepdims=True)
    row = jnp.sum(jnp.where(u == t, column, 0.0), axis=0, keepdims=True)
    return column, row


def summary_kernel(q_ref, c_ref, ld_ref, out_ref):
    column, _ = log_sums(ld_ref[...])
    grow = jnp.exp(column)
    total = jnp.zeros((E, E), F32)
    for r in range(2):
        cols = slice(r * E, (r + 1) * E)
        half = c_ref[:, cols].astype(F32) * 0.5
        total += mm(q_ref[:, cols], (grow * half).astype(BF16), TN)
    last = jnp.broadcast_to(column[LEN - 1 :, :], (8, E))
    for m in range(NP):
        out_ref[m ^ FIRST, :ROWS, :] = total[m * ROWS : (m + 1) * ROWS] * LIN
        out_ref[m ^ FIRST, ROWS:, :] = last


def summary(q, c, ld):
    return pl.pallas_call(
        summary_kernel,
        out_shape=jax.ShapeDtypeStruct((NP, ROWS + 8, E), F32),
        in_specs=vmem(3),
        out_specs=vmem(1)[0],
        cost_estimate=cost(2 * LEN * E * E * 2, 400000),
        compiler_params=params(60),
        name="summary",
    )(q, c, ld)


def pair_kernel(own_ref, got_ref, ld_ref, out_ref):
    for i, ref in enumerate((own_ref, got_ref)):
        rows = ref[...].T.reshape(NH * NY, NC, 16, LEN)
        for core in range(NC):
            out_ref[i, core] = rows[:, core].reshape(XD // NC, LEN)


def pair_up(own, got, ld):
    return pl.pallas_call(
        pair_kernel,
        out_shape=jax.ShapeDtypeStruct((2, NC, XD // NC, LEN), BF16),
        in_specs=vmem(3),
        out_specs=vmem(1)[0],
        cost_estimate=cost(0, 1000000),
        compiler_params=params(8),
        name="pair_up",
    )(own, got, ld)


def local_kernel(idx_ref, q_ref, c_ref, k_ref, v_ref, prior_ref, ld_ref, own_ref, back_ref, tail_ref):
    column, row = log_sums(ld_ref[...])
    j = lax.broadcasted_iota(jnp.int32, (LEN, LEN), 0)
    t = lax.broadcasted_iota(jnp.int32, (LEN, LEN), 1)
    inside = j <= t
    mixing = jnp.exp(jnp.where(inside, row - column, neg_fill))
    outside = jnp.where(idx_ref[0] > 0, 0.0, neg_fill)
    k, v = k_ref[...], v_ref[...]
    prior_k, prior_v = prior_ref[:, :E], prior_ref[:, E:]
    own_k, own_v = jnp.zeros((LEN, E), F32), jnp.zeros((LEN, E), F32)
    win_k, win_v = jnp.zeros((LEN, E), F32), jnp.zeros((LEN, E), F32)
    old_k, old_v = jnp.zeros((LEN, E), F32), jnp.zeros((LEN, E), F32)
    zero = jnp.zeros((LEN, LEN), BF16)
    for r in range(2):
        cols = slice(r * E, (r + 1) * E)
        q = q_ref[:, cols]
        half = (c_ref[:, cols].astype(F32) * 0.5).astype(BF16)
        raw = mm(k, q, NT)
        prod = mm(v, half, NT)
        scores = jnp.where(inside, raw, mm(prior_k, q, NT) + outside) * FACTOR
        dprob = jnp.where(inside, prod, mm(prior_v, half, NT))
        expo = jnp.exp(scores - jnp.max(scores, axis=0, keepdims=True))
        attend = expo * (1.0 / jnp.sum(expo, axis=0, keepdims=True))
        delta = jnp.sum(attend * dprob, axis=0, keepdims=True)
        dscore = (attend * (dprob - delta)).astype(BF16)
        low = attend.astype(BF16)
        own_k += mm((mixing * prod).astype(BF16), q, NN)
        own_v += mm((mixing * raw).astype(BF16), half, NN)
        win_k += mm(jnp.where(inside, dscore, zero), q, NN)
        win_v += mm(jnp.where(inside, low, zero), half, NN)
        old_k += mm(jnp.where(inside, zero, dscore), q, NN)
        old_v += mm(jnp.where(inside, zero, low), half, NN)
    own_ref[:, :E] = own_k * LIN + win_k * FACTOR
    own_ref[:, E:] = own_v * LIN + win_v
    back_ref[:, :E] = old_k * FACTOR
    back_ref[:, E:] = old_v
    tail_ref[...] = jnp.broadcast_to(jnp.exp(column[LEN - 1 :, :] - column), (LEN, E))


def local(idx, q, c, k, v, prior, ld):
    shape = jax.ShapeDtypeStruct((LEN, 2 * E), F32)
    return pl.pallas_call(
        local_kernel,
        out_shape=(shape, shape, jax.ShapeDtypeStruct((LEN, E), F32)),
        in_specs=[SMEM] + vmem(6),
        out_specs=tuple(vmem(3)),
        cost_estimate=cost(2 * 20 * LEN * LEN * E, 1200000),
        compiler_params=params(16),
        name="local",
    )(idx, q, c, k, v, prior, ld)


def plane_kernel(got_ref, out_ref):
    log = jnp.zeros((8, E), F32)
    low, high = jnp.zeros((8, E), F32), jnp.zeros((8, E), F32)
    for k in range(NP):
        weight = jnp.exp(log)
        low += weight * got_ref[k ^ FIRST, 0:8, :]
        high += weight * got_ref[k ^ FIRST, 8:16, :]
        log += got_ref[k ^ FIRST, ROWS:, :]
    row = lax.broadcasted_iota(jnp.int32, (8, E), 0)
    first = log.astype(BF16).astype(F32)
    second = (log - first).astype(BF16).astype(F32)
    third = log - first - second
    terms = jnp.where(row == 0, first, jnp.where(row == 1, second, jnp.where(row == 2, third, 0.0)))
    sent = jnp.concatenate([low, high, terms], axis=0).astype(BF16)
    for z in range(NZ):
        out_ref[z] = sent


def plane_total(got):
    return pl.pallas_call(
        plane_kernel,
        out_shape=jax.ShapeDtypeStruct((NZ, ROWS + 8, E), BF16),
        in_specs=vmem(1),
        out_specs=vmem(1)[0],
        cost_estimate=cost(0, 300000),
        compiler_params=params(4),
        name="plane_total",
    )(got)


def enter_kernel(idx_ref, got_ref, planes_ref, out_ref):
    mine = lax.div(idx_ref[0], jnp.int32(NP))
    log = jnp.zeros((1, E), F32)
    state = jnp.zeros((ROWS, E), F32)
    for z in range(NZ):
        later = z > mine
        plane = planes_ref[z ^ ACROSS].astype(F32)
        state += jnp.where(later, jnp.exp(log), 0.0) * plane[:ROWS]
        log += jnp.where(later, jnp.sum(plane[ROWS:], axis=0, keepdims=True), 0.0)
    for k in range(NP - 1, -1, -1):
        out_ref[k ^ LAST] = state
        block = got_ref[k ^ FIRST]
        state = block[:ROWS] + jnp.exp(block[ROWS : ROWS + 1]) * state


def enter(idx, got, planes):
    return pl.pallas_call(
        enter_kernel,
        out_shape=jax.ShapeDtypeStruct((NP, ROWS, E), F32),
        in_specs=[SMEM] + vmem(2),
        out_specs=vmem(1)[0],
        cost_estimate=cost(0, 400000),
        compiler_params=params(4),
        name="enter",
    )(idx, got, planes)


def half_weights(near_ref, far_ref, grad, core, head, write):
    for i in range(NH):
        x = (near_ref if i < 2 else far_ref)[i % 2, core]
        found = mm(x, grad, NN).reshape(NH // NB, NB, NY, 16, 2 * E)
        shard = lax.bitwise_xor(head, jnp.int32((0, 2, 1, 3)[i]))
        count = NH // NB
        where = pl.ds(lax.bitwise_xor(shard, jnp.int32(FAR // count)) * count, count)
        for b in range(NB):
            for y in range(NY):
                write((b * NY + y) ^ NEAR, where, found[:, b, y])


def send_kernel(
    idx_ref, state_ref, own_ref, back_ref, k_ref, v_ref, tail_ref, near_ref, far_ref, send_ref, grad_ref
):
    state = jnp.concatenate([state_ref[m ^ LAST] for m in range(NP)], axis=0)
    high = state.astype(BF16)
    low = (state - high.astype(F32)).astype(BF16)
    k, v, tail = k_ref[...], v_ref[...], tail_ref[...]
    far_k = mm(v, high, NT) + mm(v, low, NT)
    far_v = mm(k, high, NN) + mm(k, low, NN)
    grad_ref[:, :E] = (own_ref[:, :E] + back_ref[:, :E] + tail * far_k).astype(BF16)
    grad_ref[:, E:] = (own_ref[:, E:] + back_ref[:, E:] + tail * far_v).astype(BF16)

    def write(near, where, rows):
        send_ref[near, where] = rows.astype(BF16)

    half_weights(near_ref, far_ref, grad_ref[...], 1 - lax.rem(idx_ref[0], jnp.int32(NC)), idx_ref[1], write)


WHOLE = (NB * NY, NA, 16, 2 * E)


def send_half(idx, *operands):
    return pl.pallas_call(
        send_kernel,
        out_shape=(
            jax.ShapeDtypeStruct(WHOLE, BF16),
            jax.ShapeDtypeStruct((LEN, 2 * E), BF16),
        ),
        in_specs=[SMEM] + vmem(8),
        out_specs=tuple(vmem(2)),
        cost_estimate=cost(NH * XD * LEN * 2 * E, 2500000),
        compiler_params=params(16),
        name="send_half",
    )(idx, *operands)


def keep_kernel(idx_ref, grad_ref, near_ref, far_ref, keep_ref):
    def write(near, where, rows):
        keep_ref[near, where] = rows

    half_weights(near_ref, far_ref, grad_ref[...], lax.rem(idx_ref[0], jnp.int32(NC)), idx_ref[1], write)


def keep_half(idx, *operands):
    return pl.pallas_call(
        keep_kernel,
        out_shape=jax.ShapeDtypeStruct(WHOLE, F32),
        in_specs=[SMEM] + vmem(3),
        out_specs=vmem(1)[0],
        cost_estimate=cost(NH * XD * LEN * 2 * E, 2500000),
        compiler_params=params(16),
        name="keep_half",
    )(idx, *operands)


def shifted(value, steps):
    count = NZ * NP
    leading, last = (max(0, -steps), min(count, count - steps))
    return lax.ppermute(value, "ctx", [(source, source + steps) for source in range(leading, last)])


def merge_kernel(keep_ref, other_ref, out_ref):
    out_ref[...] = (keep_ref[...] + other_ref[...].astype(F32)).astype(BF16)


def merge(keep, other):
    return pl.pallas_call(
        merge_kernel,
        out_shape=jax.ShapeDtypeStruct(other.shape, BF16),
        in_specs=vmem(2),
        out_specs=vmem(1)[0],
        cost_estimate=cost(0, 2000000),
        compiler_params=params(8),
        name="merge",
    )(keep, other)


def summed(parts_ref):
    total = parts_ref[0].astype(F32)
    for i in range(1, parts_ref.shape[0]):
        total += parts_ref[i].astype(F32)
    return total


def fold_kernel(parts_ref, out_ref):
    out_ref[...] = summed(parts_ref).astype(BF16)


def fold(parts):
    return pl.pallas_call(
        fold_kernel,
        out_shape=jax.ShapeDtypeStruct(parts.shape[1:], BF16),
        in_specs=vmem(1),
        out_specs=vmem(1)[0],
        cost_estimate=cost(0, 600000),
        compiler_params=params(8),
        name="fold",
    )(parts)


def finish_kernel(parts_ref, key_ref, value_ref):
    total = summed(parts_ref)
    key_ref[...] = total[:, :E].astype(BF16)
    value_ref[...] = total[:, E:].astype(BF16)


def finish(parts):
    shape = jax.ShapeDtypeStruct((16, E), BF16)
    return pl.pallas_call(
        finish_kernel,
        out_shape=(shape, shape),
        in_specs=vmem(1),
        out_specs=tuple(vmem(2)),
        cost_estimate=cost(0, 150000),
        compiler_params=params(4),
        name="finish",
    )(parts)


def exchange(value, groups):
    return lax.all_to_all(value, "ctx", 0, 0, axis_index_groups=groups, tiled=True)


def on_device(layer_input, queries, keys, values, result_cotangent, log_decay):
    idx = jnp.stack([lax.axis_index("ctx"), lax.axis_index("head")]).astype(jnp.int32)
    sent = summary(queries, result_cotangent, log_decay)
    got = exchange(sent, plane_groups(FIRST))
    pair = jnp.concatenate([keys, values], axis=1)
    prior = shifted(pair, 1)
    opposite = lax.ppermute(layer_input, "head", [(i, i ^ 2) for i in range(NH)])
    near = pair_up(layer_input, opposite, log_decay)
    far = lax.ppermute(near, "head", [(i, i ^ 1) for i in range(NH)])
    total = plane_total(got)
    planes = exchange(total, z_groups(ACROSS))
    own, old, tail = local(idx, queries, result_cotangent, keys, values, prior, log_decay)
    back = shifted(old, -1)
    entering = enter(idx, got, planes)
    state = exchange(entering, plane_groups(LAST))
    send, grad = send_half(idx, state, own, back, keys, values, tail, near, far)
    other = lax.ppermute(send, "ctx", [(i, i ^ 1) for i in range(NZ * NP)])
    keep = keep_half(idx, grad, near, far)
    parts = fold(exchange(merge(keep, other), near_groups(NEAR)))
    return finish(exchange(parts, far_groups(FAR)))


def solution(mesh):
    rows = P("ctx", "head")
    in_specs = (rows, rows, rows, rows, rows, P("head", "ctx"))

    return jax.shard_map(
        on_device, mesh=mesh, in_specs=in_specs, out_specs=(rows, rows), check_vma=False
    )
```

```python
import jax
import jax.numpy as jnp
from jax import lax
from jax.experimental import pallas as pl
from jax.experimental.pallas import tpu as pltpu
from jax.sharding import PartitionSpec as P


E = 128
LEN = 256
NA, NB, NY, NC = 8, 2, 4, 2
NZ = NA * NB
NP = NY * NC
NH = 4
XD = 512
ROWS = E // NP
LIN = 1.0 / (32 * E)
FACTOR = E ** (-0.5)
F32, BF16 = jnp.float32, jnp.bfloat16

neg_fill = -1e30


FIRST, ACROSS, LAST, NEAR, FAR = 5, 10, 1, 6, 4


def place(z, y, core):
    return (z * NY + y) * NC + core


def plane_groups(lead):
    return [[z * NP + (q ^ lead) for q in range(NP)] for z in range(NZ)]


def z_groups(lead):
    return [[(q + lead) % NZ * NP + p for q in range(NZ)] for p in range(NP)]


def near_groups(lead):
    members = [(q + lead) % (NB * NY) for q in range(NB * NY)]
    return [
        [place(a * NB + m // NY, m % NY, core) for m in members]
        for a in range(NA)
        for core in range(NC)
    ]


def far_groups(lead):
    return [
        [place((q ^ lead) * NB + b, y, core) for q in range(NA)]
        for b in range(NB)
        for y in range(NY)
        for core in range(NC)
    ]


NN = (((1,), (0,)), ((), ()))
NT = (((1,), (1,)), ((), ()))
TN = (((0,), (0,)), ((), ()))


def mm(a, b, dims):
    return lax.dot_general(a, b, dims, preferred_element_type=F32)


def vmem(count):
    return [pl.BlockSpec(memory_space=pltpu.VMEM)] * count


SMEM = pl.BlockSpec(memory_space=pltpu.SMEM)


def cost(flops, nbytes):
    return pl.CostEstimate(flops=flops, bytes_accessed=nbytes, transcendentals=0)


def params(mib):
    return pltpu.CompilerParams(vmem_limit_bytes=mib << 20)


def log_sums(ld):
    t = lax.broadcasted_iota(jnp.int32, (LEN, LEN), 0)
    u = lax.broadcasted_iota(jnp.int32, (LEN, LEN), 1)
    column = jnp.sum(jnp.where(u <= t, ld, 0.0), axis=1, keepdims=True)
    row = jnp.sum(jnp.where(u == t, column, 0.0), axis=0, keepdims=True)
    return column, row


def summary_kernel(q_ref, c_ref, ld_ref, out_ref):
    column, _ = log_sums(ld_ref[...])
    grow = jnp.exp(column)
    total = jnp.zeros((E, E), F32)
    for r in range(2):
        cols = slice(r * E, (r + 1) * E)
        half = c_ref[:, cols].astype(F32) * 0.5
        total += mm(q_ref[:, cols], (grow * half).astype(BF16), TN)
    last = jnp.broadcast_to(column[LEN - 1 :, :], (8, E))
    for m in range(NP):
        out_ref[m ^ FIRST, :ROWS, :] = total[m * ROWS : (m + 1) * ROWS] * LIN
        out_ref[m ^ FIRST, ROWS:, :] = last


def summary(q, c, ld):
    return pl.pallas_call(
        summary_kernel,
        out_shape=jax.ShapeDtypeStruct((NP, ROWS + 8, E), F32),
        in_specs=vmem(3),
        out_specs=vmem(1)[0],
        cost_estimate=cost(2 * LEN * E * E * 2, 400000),
        compiler_params=params(60),
        name="summary",
    )(q, c, ld)


def pair_kernel(own_ref, got_ref, ld_ref, out_ref):
    for i, ref in enumerate((own_ref, got_ref)):
        rows = ref[...].T.reshape(NH * NY, NC, 16, LEN)
        for core in range(NC):
            out_ref[i, core] = rows[:, core].reshape(XD // NC, LEN)


def pair_up(own, got, ld):
    return pl.pallas_call(
        pair_kernel,
        out_shape=jax.ShapeDtypeStruct((2, NC, XD // NC, LEN), BF16),
        in_specs=vmem(3),
        out_specs=vmem(1)[0],
        cost_estimate=cost(0, 1000000),
        compiler_params=params(8),
        name="pair_up",
    )(own, got, ld)


def local_kernel(idx_ref, q_ref, c_ref, k_ref, v_ref, prior_ref, ld_ref, own_ref, back_ref, tail_ref):
    column, row = log_sums(ld_ref[...])
    j = lax.broadcasted_iota(jnp.int32, (LEN, LEN), 0)
    t = lax.broadcasted_iota(jnp.int32, (LEN, LEN), 1)
    inside = j <= t
    mixing = jnp.exp(jnp.where(inside, row - column, neg_fill))
    outside = jnp.where(idx_ref[0] > 0, 0.0, neg_fill)
    k, v = k_ref[...], v_ref[...]
    prior_k, prior_v = prior_ref[:, :E], prior_ref[:, E:]
    own_k, own_v = jnp.zeros((LEN, E), F32), jnp.zeros((LEN, E), F32)
    win_k, win_v = jnp.zeros((LEN, E), F32), jnp.zeros((LEN, E), F32)
    old_k, old_v = jnp.zeros((LEN, E), F32), jnp.zeros((LEN, E), F32)
    zero = jnp.zeros((LEN, LEN), BF16)
    for r in range(2):
        cols = slice(r * E, (r + 1) * E)
        q = q_ref[:, cols]
        half = (c_ref[:, cols].astype(F32) * 0.5).astype(BF16)
        raw = mm(k, q, NT)
        prod = mm(v, half, NT)
        scores = jnp.where(inside, raw, mm(prior_k, q, NT) + outside) * FACTOR
        dprob = jnp.where(inside, prod, mm(prior_v, half, NT))
        expo = jnp.exp(scores - jnp.max(scores, axis=0, keepdims=True))
        attend = expo * (1.0 / jnp.sum(expo, axis=0, keepdims=True))
        delta = jnp.sum(attend * dprob, axis=0, keepdims=True)
        dscore = (attend * (dprob - delta)).astype(BF16)
        low = attend.astype(BF16)
        own_k += mm((mixing * prod).astype(BF16), q, NN)
        own_v += mm((mixing * raw).astype(BF16), half, NN)
        win_k += mm(jnp.where(inside, dscore, zero), q, NN)
        win_v += mm(jnp.where(inside, low, zero), half, NN)
        old_k += mm(jnp.where(inside, zero, dscore), q, NN)
        old_v += mm(jnp.where(inside, zero, low), half, NN)
    own_ref[:, :E] = own_k * LIN + win_k * FACTOR
    own_ref[:, E:] = own_v * LIN + win_v
    back_ref[:, :E] = old_k * FACTOR
    back_ref[:, E:] = old_v
    tail_ref[...] = jnp.broadcast_to(jnp.exp(column[LEN - 1 :, :] - column), (LEN, E))


def local(idx, q, c, k, v, prior, ld):
    shape = jax.ShapeDtypeStruct((LEN, 2 * E), F32)
    return pl.pallas_call(
        local_kernel,
        out_shape=(shape, shape, jax.ShapeDtypeStruct((LEN, E), F32)),
        in_specs=[SMEM] + vmem(6),
        out_specs=tuple(vmem(3)),
        cost_estimate=cost(2 * 20 * LEN * LEN * E, 1200000),
        compiler_params=params(16),
        name="local",
    )(idx, q, c, k, v, prior, ld)


def plane_kernel(got_ref, out_ref):
    log = jnp.zeros((8, E), F32)
    low, high = jnp.zeros((8, E), F32), jnp.zeros((8, E), F32)
    for k in range(NP):
        weight = jnp.exp(log)
        low += weight * got_ref[k ^ FIRST, 0:8, :]
        high += weight * got_ref[k ^ FIRST, 8:16, :]
        log += got_ref[k ^ FIRST, ROWS:, :]
    row = lax.broadcasted_iota(jnp.int32, (8, E), 0)
    first = log.astype(BF16).astype(F32)
    second = (log - first).astype(BF16).astype(F32)
    third = log - first - second
    terms = jnp.where(row == 0, first, jnp.where(row == 1, second, jnp.where(row == 2, third, 0.0)))
    sent = jnp.concatenate([low, high, terms], axis=0).astype(BF16)
    for z in range(NZ):
        out_ref[z] = sent


def plane_total(got):
    return pl.pallas_call(
        plane_kernel,
        out_shape=jax.ShapeDtypeStruct((NZ, ROWS + 8, E), BF16),
        in_specs=vmem(1),
        out_specs=vmem(1)[0],
        cost_estimate=cost(0, 300000),
        compiler_params=params(4),
        name="plane_total",
    )(got)


def enter_kernel(idx_ref, got_ref, planes_ref, out_ref):
    mine = lax.div(idx_ref[0], jnp.int32(NP))
    log = jnp.zeros((1, E), F32)
    state = jnp.zeros((ROWS, E), F32)
    for z in range(NZ):
        later = z > mine
        plane = planes_ref[(z - ACROSS) % NZ].astype(F32)
        state += jnp.where(later, jnp.exp(log), 0.0) * plane[:ROWS]
        log += jnp.where(later, jnp.sum(plane[ROWS:], axis=0, keepdims=True), 0.0)
    for k in range(NP - 1, -1, -1):
        out_ref[k ^ LAST] = state
        block = got_ref[k ^ FIRST]
        state = block[:ROWS] + jnp.exp(block[ROWS : ROWS + 1]) * state


def enter(idx, got, planes):
    return pl.pallas_call(
        enter_kernel,
        out_shape=jax.ShapeDtypeStruct((NP, ROWS, E), F32),
        in_specs=[SMEM] + vmem(2),
        out_specs=vmem(1)[0],
        cost_estimate=cost(0, 400000),
        compiler_params=params(4),
        name="enter",
    )(idx, got, planes)


def half_weights(near_ref, far_ref, grad, core, head, write):
    for i in range(NH):
        x = (near_ref if i < 2 else far_ref)[i % 2, core]
        found = mm(x, grad, NN).reshape(NH // NB, NB, NY, 16, 2 * E)
        shard = lax.bitwise_xor(head, jnp.int32((0, 2, 1, 3)[i]))
        count = NH // NB
        where = pl.ds(lax.bitwise_xor(shard, jnp.int32(FAR // count)) * count, count)
        for b in range(NB):
            for y in range(NY):
                write((b * NY + y - NEAR) % (NB * NY), where, found[:, b, y])


def send_kernel(
    idx_ref, state_ref, own_ref, back_ref, k_ref, v_ref, tail_ref, near_ref, far_ref, send_ref, grad_ref
):
    state = jnp.concatenate([state_ref[m ^ LAST] for m in range(NP)], axis=0)
    high = state.astype(BF16)
    low = (state - high.astype(F32)).astype(BF16)
    k, v, tail = k_ref[...], v_ref[...], tail_ref[...]
    far_k = mm(v, high, NT) + mm(v, low, NT)
    far_v = mm(k, high, NN) + mm(k, low, NN)
    grad_ref[:, :E] = (own_ref[:, :E] + back_ref[:, :E] + tail * far_k).astype(BF16)
    grad_ref[:, E:] = (own_ref[:, E:] + back_ref[:, E:] + tail * far_v).astype(BF16)

    def write(near, where, rows):
        send_ref[near, where] = rows.astype(BF16)

    half_weights(near_ref, far_ref, grad_ref[...], 1 - lax.rem(idx_ref[0], jnp.int32(NC)), idx_ref[1], write)


WHOLE = (NB * NY, NA, 16, 2 * E)


def send_half(idx, *operands):
    return pl.pallas_call(
        send_kernel,
        out_shape=(
            jax.ShapeDtypeStruct(WHOLE, BF16),
            jax.ShapeDtypeStruct((LEN, 2 * E), BF16),
        ),
        in_specs=[SMEM] + vmem(8),
        out_specs=tuple(vmem(2)),
        cost_estimate=cost(NH * XD * LEN * 2 * E, 2500000),
        compiler_params=params(16),
        name="send_half",
    )(idx, *operands)


def keep_kernel(idx_ref, grad_ref, near_ref, far_ref, keep_ref):
    def write(near, where, rows):
        keep_ref[near, where] = rows

    half_weights(near_ref, far_ref, grad_ref[...], lax.rem(idx_ref[0], jnp.int32(NC)), idx_ref[1], write)


def keep_half(idx, *operands):
    return pl.pallas_call(
        keep_kernel,
        out_shape=jax.ShapeDtypeStruct(WHOLE, F32),
        in_specs=[SMEM] + vmem(3),
        out_specs=vmem(1)[0],
        cost_estimate=cost(NH * XD * LEN * 2 * E, 2500000),
        compiler_params=params(16),
        name="keep_half",
    )(idx, *operands)


def shifted(value, steps):
    count = NZ * NP
    leading, last = (max(0, -steps), min(count, count - steps))
    return lax.ppermute(value, "ctx", [(source, source + steps) for source in range(leading, last)])


def merge_kernel(keep_ref, other_ref, out_ref):
    out_ref[...] = (keep_ref[...] + other_ref[...].astype(F32)).astype(BF16)


def merge(keep, other):
    return pl.pallas_call(
        merge_kernel,
        out_shape=jax.ShapeDtypeStruct(other.shape, BF16),
        in_specs=vmem(2),
        out_specs=vmem(1)[0],
        cost_estimate=cost(0, 2000000),
        compiler_params=params(8),
        name="merge",
    )(keep, other)


def summed(parts_ref):
    total = parts_ref[0].astype(F32)
    for i in range(1, parts_ref.shape[0]):
        total += parts_ref[i].astype(F32)
    return total


def fold_kernel(parts_ref, out_ref):
    out_ref[...] = summed(parts_ref).astype(BF16)


def fold(parts):
    return pl.pallas_call(
        fold_kernel,
        out_shape=jax.ShapeDtypeStruct(parts.shape[1:], BF16),
        in_specs=vmem(1),
        out_specs=vmem(1)[0],
        cost_estimate=cost(0, 600000),
        compiler_params=params(8),
        name="fold",
    )(parts)


def finish_kernel(parts_ref, key_ref, value_ref):
    total = summed(parts_ref)
    key_ref[...] = total[:, :E].astype(BF16)
    value_ref[...] = total[:, E:].astype(BF16)


def finish(parts):
    shape = jax.ShapeDtypeStruct((16, E), BF16)
    return pl.pallas_call(
        finish_kernel,
        out_shape=(shape, shape),
        in_specs=vmem(1),
        out_specs=tuple(vmem(2)),
        cost_estimate=cost(0, 150000),
        compiler_params=params(4),
        name="finish",
    )(parts)


def exchange(value, groups):
    return lax.all_to_all(value, "ctx", 0, 0, axis_index_groups=groups, tiled=True)


def on_device(layer_input, queries, keys, values, result_cotangent, log_decay):
    idx = jnp.stack([lax.axis_index("ctx"), lax.axis_index("head")]).astype(jnp.int32)
    sent = summary(queries, result_cotangent, log_decay)
    got = exchange(sent, plane_groups(FIRST))
    pair = jnp.concatenate([keys, values], axis=1)
    prior = shifted(pair, 1)
    opposite = lax.ppermute(layer_input, "head", [(i, i ^ 2) for i in range(NH)])
    near = pair_up(layer_input, opposite, log_decay)
    far = lax.ppermute(near, "head", [(i, i ^ 1) for i in range(NH)])
    total = plane_total(got)
    planes = exchange(total, z_groups(ACROSS))
    own, old, tail = local(idx, queries, result_cotangent, keys, values, prior, log_decay)
    back = shifted(old, -1)
    entering = enter(idx, got, planes)
    state = exchange(entering, plane_groups(LAST))
    send, grad = send_half(idx, state, own, back, keys, values, tail, near, far)
    other = lax.ppermute(send, "ctx", [(i, i ^ 1) for i in range(NZ * NP)])
    keep = keep_half(idx, grad, near, far)
    parts = fold(exchange(merge(keep, other), near_groups(NEAR)))
    return finish(exchange(parts, far_groups(FAR)))


def solution(mesh):
    rows = P("ctx", "head")
    in_specs = (rows, rows, rows, rows, rows, P("head", "ctx"))

    return jax.shard_map(
        on_device, mesh=mesh, in_specs=in_specs, out_specs=(rows, rows), check_vma=False
    )
```
